512 devices in a mesh: dp: 64 (over x, y, z_lo), uly: 8 (over z_hi, core).
Axes of the slice: x: 4, y: 8, z: 8 (z_hi: 4, z_lo: 2; z = z_hi * 2 + z_lo), core: 2. Of those that a mesh axis runs over, the one named last changes fastest.
Arguments:
- hidden_in: bfloat16 [64, 1024, 8192], P('dp', 'uly'), may hold values from -6 to 6
- queries: bfloat16 [64, 1024, 4096], P('dp', 'uly'), may hold values from -6 to 6
- keys: bfloat16 [64, 1024, 512], P('dp', 'uly'), may hold values from -6 to 6
- values: bfloat16 [64, 1024, 512], P('dp', 'uly'), may hold values from -6 to 6
- out_grad: bfloat16 [64, 1024, 4096], P('dp', 'uly'), may hold values from -6 to 6
- doc_ids: int32 [64, 1024], P('dp', 'uly'), may hold values from 0 to 2, never falling along the last dimension, each value on 1 to 512 neighbouring positions
- flora_proj: bfloat16 [8192, 256], P('uly'), may hold values from -0.0078125 to 0.0078125
Outputs:
- flora_q: float32 [256, 4096], P('dp', 'uly')
- flora_k: float32 [256, 512], P('dp', 'uly')
- flora_v: float32 [256, 512], P('dp', 'uly')
The draws below stay inside these ranges and needn't reach their ends.
All inputs are finite; a program needn't handle non-finite values.
Results may differ from the reference program's by a relative error of at most 0.0076.
Values may be sent and summed in bfloat16 or wider, within the bound.
No kernel may reach another device: no remote copies, remote signals or barrier semaphores. Data moves between devices by JAX's collectives and lax.ppermute only.
A program may use at most 64 MiB of HBM per device.

```python
import math
import jax
import jax.numpy as jnp
import numpy as np
from jax import lax

D = 8192
QUERY_HEADS = 32
KEY_VALUE_HEADS = 4
HEAD_SIZE = 128
FLORA_RANK = 256
DOCS = 3
SEQUENCE_LENGTH = 1024
SEQUENCE_COUNT = 64


def draw_queries(key, part):
    start_offset = jnp.clip(jax.random.normal(jax.random.fold_in(key, 11), (SEQUENCE_COUNT, SEQUENCE_LENGTH, QUERY_HEADS * HEAD_SIZE), jnp.float32), -6.0, 6.0)
    return start_offset.astype(jnp.bfloat16)


def draw_keys(key, part):
    start_offset = jnp.clip(jax.random.normal(jax.random.fold_in(key, 17), (SEQUENCE_COUNT, SEQUENCE_LENGTH, KEY_VALUE_HEADS * HEAD_SIZE), jnp.float32), -6.0, 6.0)
    return start_offset.astype(jnp.bfloat16)


def levels(own_key, extent, pieces, low, largest):
    factor_of, own = 1.0, jax.random.fold_in(own_key, 6)
    for dim, shards_of in pieces:
        steps = jnp.exp(jax.random.uniform(jax.random.fold_in(own, dim), (shards_of,), jnp.float32, low / len(pieces), largest / len(pieces)))
        factor_of = factor_of * jnp.repeat(steps, extent[dim] // shards_of).reshape([-1 if axis == dim else 1 for axis in range(len(extent))])
    return factor_of


def profile(number_of, total, reach, slope):
    loads = [(1 << 20) // math.isqrt(rank ** slope) + 1 for rank in range(2, number_of + 1)]
    rest, given = total - reach - (number_of - 1), [1] * (number_of - 1)
    while rest > 0:
        candidates = [i for i in range(number_of - 1) if given[i] < reach]
        whole, remaining = sum([loads[i] for i in candidates]), rest
        for i in candidates:
            extra = min(reach - given[i], max(1, remaining * loads[i] // whole), rest)
            given[i] = given[i] + extra
            rest = rest - extra
    return np.array([reach] + given)


def ragged_sizes(key, amount, total, most, lean):
    if amount == 2:
        one = jax.random.randint(key, (), max(1, total - most), min(most, total - 1) + 1)
        return jnp.stack([one, total - one])
    tallies = jnp.asarray(profile(amount, total, most, lean), jnp.int32)
    pairs = (amount - 1) // 2
    source_of, receiver = tallies[1:1 + 2 * pairs:2], tallies[2:2 + 2 * pairs:2]
    margin = jnp.minimum(source_of - 1, most - receiver)
    passed = jax.random.randint(jax.random.fold_in(key, 1), (pairs,), 0, 1 << 20) % (margin + 1)
    tallies = tallies.at[1:1 + 2 * pairs:2].set(source_of - passed).at[2:2 + 2 * pairs:2].set(receiver + passed)
    return tallies[jax.random.permutation(jax.random.fold_in(key, 2), amount)]


def bell_draw(stream_key, dims, deviation, limit, cuts=(), kind=jnp.bfloat16):
    drawn = deviation * jax.random.normal(stream_key, dims, jnp.float32)
    if cuts:
        drawn = drawn * levels(stream_key, dims, cuts, -0.22, 0.18)
    return jnp.clip(drawn, -limit, limit).astype(kind)


def setup_inputs(seed: int = 0) -> dict:
    arg_keys = jax.random.split(jax.random.key(seed), 8)
    hidden_in = bell_draw(arg_keys[0], (SEQUENCE_COUNT, SEQUENCE_LENGTH, D), 1.0, 6.0, ((0, 64), (1, 8)))
    queries = draw_queries(jax.random.fold_in(arg_keys[7], 71), 0)
    keys = draw_keys(jax.random.fold_in(arg_keys[7], 71), 0)
    values = bell_draw(arg_keys[3], (SEQUENCE_COUNT, SEQUENCE_LENGTH, KEY_VALUE_HEADS * HEAD_SIZE), 1.0, 6.0, ((0, 64), (1, 8)))
    out_grad = bell_draw(arg_keys[4], (SEQUENCE_COUNT, SEQUENCE_LENGTH, QUERY_HEADS * HEAD_SIZE), 1.0, 6.0, ((0, 64), (1, 8)))
    doc_ids = jax.vmap(lambda own: jnp.searchsorted(jnp.cumsum(ragged_sizes(own, DOCS, SEQUENCE_LENGTH, SEQUENCE_LENGTH // 2, 0)), jnp.arange(SEQUENCE_LENGTH), side="right"))(jax.random.split(arg_keys[5], SEQUENCE_COUNT)).reshape((SEQUENCE_COUNT, SEQUENCE_LENGTH)).astype(jnp.int32)
    flora_proj = bell_draw(arg_keys[6], (D, FLORA_RANK), (D * SEQUENCE_COUNT) ** -0.5, 0.0078125, ((0, 8),))
    return dict(hidden_in=hidden_in, queries=queries, keys=keys, values=values, out_grad=out_grad, doc_ids=doc_ids, flora_proj=flora_proj)


def head_grads(query_head, key_head, value_head, grad_head, segments):
    span_length = query_head.shape[0]
    inv_root = 1.0 / math.sqrt(HEAD_SIZE)
    scores = jnp.dot(query_head, key_head.T, preferred_element_type=jnp.float32) * inv_root
    positions = jnp.arange(span_length, dtype=jnp.int32)
    allowed = (positions[None, :] <= positions[:, None]) & (segments[None, :] == segments[:, None])
    scores = jnp.where(allowed, scores, -jnp.inf)
    row_peak = lax.optimization_barrier(jnp.max(scores, axis=1, keepdims=True))
    weights = jnp.exp(scores - row_peak)
    attn_probs = weights / lax.optimization_barrier(jnp.sum(weights, axis=1, keepdims=True))
    probs_low = attn_probs.astype(jnp.bfloat16)
    attended = jnp.dot(probs_low, value_head, preferred_element_type=jnp.float32)
    row_delta = lax.optimization_barrier(jnp.sum(grad_head.astype(jnp.float32) * attended, axis=1, keepdims=True))
    grad_probs = jnp.dot(grad_head, value_head.T, preferred_element_type=jnp.float32)
    grad_scores = (attn_probs * (grad_probs - row_delta)).astype(jnp.bfloat16)
    grad_query = (jnp.dot(grad_scores, key_head, preferred_element_type=jnp.float32) * inv_root).astype(jnp.bfloat16)
    key_gradient = jnp.dot(grad_scores.T, query_head, preferred_element_type=jnp.float32) * inv_root
    value_gradient = jnp.dot(probs_low.T, grad_head, preferred_element_type=jnp.float32)
    return (grad_query, key_gradient, value_gradient)

def dim_major(matrix):
    rows_total = matrix.shape[0]
    return matrix.reshape(rows_total, KEY_VALUE_HEADS, HEAD_SIZE).transpose(0, 2, 1).reshape(rows_total, KEY_VALUE_HEADS * HEAD_SIZE)

def reference(hidden_in, queries, keys, values, out_grad, doc_ids, flora_proj):
    group_width = QUERY_HEADS // KEY_VALUE_HEADS
    span_length = queries.shape[1]

    def per_sequence(carry, inputs):
        grad_q_acc, grad_k_acc, grad_v_acc = carry
        hidden_seq, query_seq, key_sequence, value_sequence, grad_seq, segments = inputs
        projected = jnp.dot(hidden_seq, flora_proj, preferred_element_type=jnp.float32).astype(jnp.bfloat16)
        query_heads = query_seq.reshape(span_length, QUERY_HEADS, HEAD_SIZE).transpose(1, 0, 2)
        grad_heads = grad_seq.reshape(span_length, QUERY_HEADS, HEAD_SIZE).transpose(1, 0, 2)
        key_head_rows = key_sequence.reshape(span_length, KEY_VALUE_HEADS, HEAD_SIZE).transpose(1, 0, 2)
        value_head_rows = value_sequence.reshape(span_length, KEY_VALUE_HEADS, HEAD_SIZE).transpose(1, 0, 2)

        def per_head(unused, head_inputs):
            head_index, query_head, grad_head = head_inputs
            kv_index = head_index // group_width
            result = head_grads(query_head, key_head_rows[kv_index], value_head_rows[kv_index], grad_head, segments)
            return (unused, result)
        unused_carry, head_results = lax.scan(per_head, jnp.zeros((), jnp.float32), (jnp.arange(QUERY_HEADS, dtype=jnp.int32), query_heads, grad_heads))
        grad_query, key_gradient, value_gradient = head_results
        grad_query = grad_query.transpose(1, 0, 2).reshape(span_length, QUERY_HEADS * HEAD_SIZE)
        key_gradient = key_gradient.reshape(KEY_VALUE_HEADS, group_width, span_length, HEAD_SIZE).sum(axis=1).transpose(1, 0, 2).reshape(span_length, KEY_VALUE_HEADS * HEAD_SIZE)
        value_gradient = value_gradient.reshape(KEY_VALUE_HEADS, group_width, span_length, HEAD_SIZE).sum(axis=1).transpose(1, 0, 2).reshape(span_length, KEY_VALUE_HEADS * HEAD_SIZE)
        grad_q_acc = grad_q_acc + jnp.dot(projected.T, grad_query, preferred_element_type=jnp.float32)
        projected_wide = projected.astype(jnp.float32)
        grad_k_acc = grad_k_acc + jnp.dot(projected_wide.T, key_gradient, precision=lax.Precision.HIGHEST)
        grad_v_acc = grad_v_acc + jnp.dot(projected_wide.T, value_gradient, precision=lax.Precision.HIGHEST)
        return ((grad_q_acc, grad_k_acc, grad_v_acc), None)
    starting_state = (jnp.zeros((FLORA_RANK, QUERY_HEADS * HEAD_SIZE), jnp.float32), jnp.zeros((FLORA_RANK, KEY_VALUE_HEADS * HEAD_SIZE), jnp.float32), jnp.zeros((FLORA_RANK, KEY_VALUE_HEADS * HEAD_SIZE), jnp.float32))
    totals, unused_out = lax.scan(per_sequence, starting_state, (hidden_in, queries, keys, values, out_grad, doc_ids))
    flora_q, flora_k, flora_v = totals
    return (flora_q, dim_major(flora_k), dim_major(flora_v))
```

```python
import math

import jax
import jax.numpy as jnp
import numpy as np
from jax import lax
from jax.experimental import pallas as pl
from jax.experimental.pallas import tpu as pltpu
from jax.sharding import Mesh
from jax.sharding import PartitionSpec as P


HEAD = 128
ROWS = 128
RANK = 256
SEQ = 1024
BLOCKS = SEQ // ROWS
BAND = 640
INV_ROOT = 1.0 / math.sqrt(HEAD)
EXP2_SCALE = INV_ROOT * math.log2(math.e)
FIRST_HEADS = 2
HEADS = 4
TAIL = 16

NT = (((1,), (1,)), ((), ()))
TN = (((0,), (0,)), ((), ()))
NN = (((1,), (0,)), ((), ()))


def dot(a, b, dims):
    return lax.dot_general(a, b, dims, preferred_element_type=jnp.float32)


def full(shape):
    return pl.BlockSpec(shape, lambda *_: (0,) * len(shape))


SMEM = pl.BlockSpec(memory_space=pltpu.SMEM)


def pack_body(q_ref, g_ref, k_ref, v_ref, ids_ref, first_ref, second_ref):
    peer = pl.program_id(0)
    n1, n2 = FIRST_HEADS, HEADS - FIRST_HEADS
    for h in range(n1):
        cols = slice(h * HEAD, (h + 1) * HEAD)
        first_ref[0, h * ROWS : (h + 1) * ROWS, :] = q_ref[0, :, cols]
        first_ref[0, (n1 + h) * ROWS : (n1 + h + 1) * ROWS, :] = g_ref[0, :, cols]
    base = 2 * n1 * ROWS
    first_ref[0, base : base + ROWS, :] = jnp.where(peer % 2 == 0, k_ref[0], v_ref[0])
    first_ref[0, base + ROWS : base + ROWS + TAIL, :] = jnp.broadcast_to(
        ids_ref[...].astype(jnp.float32), (TAIL, ROWS)
    ).astype(jnp.bfloat16)
    for h in range(n2):
        cols = slice((n1 + h) * HEAD, (n1 + h + 1) * HEAD)
        second_ref[0, h * ROWS : (h + 1) * ROWS, :] = q_ref[0, :, cols]
        second_ref[0, (n2 + h) * ROWS : (n2 + h + 1) * ROWS, :] = g_ref[0, :, cols]


def pack(queries, out_grad, keys, values, ids):
    r1 = 2 * FIRST_HEADS * ROWS + ROWS + TAIL
    r2 = 2 * (HEADS - FIRST_HEADS) * ROWS
    wide = pl.BlockSpec((1, ROWS, HEADS * HEAD), lambda u: (0, 0, u))
    thin = pl.BlockSpec((1, ROWS, HEAD), lambda u: (0, 0, u // 2))
    return pl.pallas_call(
        pack_body,
        grid=(8,),
        in_specs=[wide, wide, thin, thin, full((1, ROWS))],
        out_specs=[
            pl.BlockSpec((1, r1, HEAD), lambda u: (u, 0, 0)),
            pl.BlockSpec((1, r2, HEAD), lambda u: (u, 0, 0)),
        ],
        out_shape=[
            jax.ShapeDtypeStruct((8, r1, HEAD), jnp.bfloat16),
            jax.ShapeDtypeStruct((8, r2, HEAD), jnp.bfloat16),
        ],
        name="pack",
    )(queries, out_grad, keys, values, ids)


def attention_body(heads, first, where_ref, qg_ref, kv_ref, other_ref, *rest):
    if first:
        gq_ref, gk_ref, gv_ref, k_sc, v_sc = rest
    else:
        gk_in, gv_in, gq_ref, gk_ref, gv_ref, k_sc, v_sc = rest
    i = pl.program_id(0)
    m_cols = heads * ROWS
    base = 2 * FIRST_HEADS * ROWS
    core = where_ref[0]

    @pl.when(i == 0)
    def _():
        if first:
            gk_ref[...] = jnp.zeros_like(gk_ref)
            gv_ref[...] = jnp.zeros_like(gv_ref)
        else:
            gk_ref[...] = gk_in[...]
            gv_ref[...] = gv_in[...]

        @pl.when(core == 0)
        def _():
            for b in range(BLOCKS):
                k_sc[b * ROWS : (b + 1) * ROWS, :] = kv_ref[b, base : base + ROWS, :]
                v_sc[b * ROWS : (b + 1) * ROWS, :] = other_ref[b]

        @pl.when(core != 0)
        def _():
            for b in range(BLOCKS):
                v_sc[b * ROWS : (b + 1) * ROWS, :] = kv_ref[b, base : base + ROWS, :]
                k_sc[b * ROWS : (b + 1) * ROWS, :] = other_ref[b]

    count0 = jnp.zeros((1, ROWS), jnp.float32)
    count1 = jnp.zeros((1, ROWS), jnp.float32)
    for b in range(BLOCKS):
        ids_b = kv_ref[b, base + ROWS : base + ROWS + TAIL, :].astype(jnp.float32)[:1]
        count0 += jnp.where(ids_b < 0.5, 1.0, 0.0)
        count1 += jnp.where(ids_b < 1.5, 1.0, 0.0)
    start1 = jnp.sum(count0, axis=1, keepdims=True).astype(jnp.int32)
    start2 = jnp.sum(count1, axis=1, keepdims=True).astype(jnp.int32)
    own_ids = kv_ref[i, base + ROWS : base + ROWS + TAIL, :].astype(jnp.float32)[:1]
    q_start = jnp.where(own_ids < 0.5, 0, jnp.where(own_ids < 1.5, start1, start2))
    q_pos = i * ROWS + lax.broadcasted_iota(jnp.int32, (1, ROWS), 1)
    q_start = jnp.concatenate([q_start] * heads, axis=1)
    q_pos = jnp.concatenate([q_pos] * heads, axis=1)

    key_start = pl.multiple_of(jnp.maximum(i - (BAND // ROWS - 1), 0) * ROWS, ROWS)
    band = pl.ds(key_start, BAND)
    k = k_sc[band, :]
    v = v_sc[band, :]
    q = qg_ref[i, : heads * ROWS, :]
    g = qg_ref[i, heads * ROWS : 2 * heads * ROWS, :]
    k_pos = key_start + lax.broadcasted_iota(jnp.int32, (BAND, m_cols), 0)
    scores = dot(k, q, NT) * EXP2_SCALE
    allowed = (k_pos <= q_pos) & (k_pos >= q_start)
    scores = jnp.where(allowed, scores, -jnp.inf)
    peak = jnp.max(scores, axis=0, keepdims=True)
    weights = jnp.exp2(scores - peak)
    inv = 1.0 / jnp.sum(weights, axis=0, keepdims=True)
    grad_probs = dot(v, g, NT)
    probs = weights * inv
    delta = jnp.sum(probs * grad_probs, axis=0, keepdims=True)
    probs_low = probs.astype(jnp.bfloat16)
    grad_scores = (probs * (grad_probs - delta)).astype(jnp.bfloat16)
    gv_ref[band, :] += dot(probs_low, g, NN)
    gk_ref[band, :] += dot(grad_scores, q, NN) * INV_ROOT
    gq = (dot(k, grad_scores, TN) * INV_ROOT).astype(jnp.bfloat16)
    for h in range(heads):
        gq_ref[:, h * HEAD : (h + 1) * HEAD] = gq[:, h * ROWS : (h + 1) * ROWS].T


def attention(heads, where, qg, kv, other, so_far=None):
    first = so_far is None
    so_far = () if first else tuple(so_far)
    wide = (SEQ, HEAD)
    return pl.pallas_call(
        lambda *refs: attention_body(heads, first, *refs),
        grid=(BLOCKS,),
        in_specs=[SMEM, full(qg.shape), full(kv.shape), full(other.shape)]
        + [full(wide)] * len(so_far),
        out_specs=[
            pl.BlockSpec((ROWS, heads * HEAD), lambda i: (i, 0)),
            full(wide),
            full(wide),
        ],
        out_shape=[
            jax.ShapeDtypeStruct((SEQ, heads * HEAD), jnp.bfloat16),
            jax.ShapeDtypeStruct(wide, jnp.float32),
            jax.ShapeDtypeStruct(wide, jnp.float32),
        ],
        scratch_shapes=[pltpu.VMEM(wide, jnp.bfloat16), pltpu.VMEM(wide, jnp.bfloat16)],
        name="attention_first" if first else "attention_rest",
    )(where, qg, kv, other, *so_far)


def project_body(where_ref, mine_ref, theirs_ref, *rest):
    pieces, (own_ref, back_ref) = rest[:8], rest[8:]
    core, x, y = where_ref[0], where_ref[2], where_ref[3]
    own = jnp.zeros((ROWS, RANK), jnp.float32)
    back = jnp.zeros((ROWS, RANK), jnp.float32)
    for ky in range(8):
        row = (y - ky + 8) % 8
        for kx in range(4):
            part = (x - kx + 4) % 4
            w = pieces[ky][kx]
            at = pl.multiple_of(((part * 2 + core) * 8 + row) * ROWS, ROWS)
            own += dot(mine_ref[0, :, pl.ds(at, ROWS)], w, NN)
            at = pl.multiple_of((part * 8 + row) * ROWS, ROWS)
            back += dot(theirs_ref[:, pl.ds(at, ROWS)], w, NN)
    own_ref[...] = own
    back_ref[...] = back


def project(where, mine, theirs, pieces):
    out = jax.ShapeDtypeStruct((ROWS, RANK), jnp.float32)
    return pl.pallas_call(
        project_body,
        in_specs=[SMEM] + [pl.BlockSpec(memory_space=pltpu.VMEM)] * (2 + len(pieces)),
        out_specs=[pl.BlockSpec(memory_space=pltpu.VMEM)] * 2,
        out_shape=[out, out],
        name="project",
    )(where, mine, theirs, *pieces)


def outer_body(where_ref, pa_ref, pb_ref, gq1_ref, gq2_ref, gk_ref, gv_ref, out_ref):
    core, zh = where_ref[0], where_ref[1]
    cols = out_ref.shape[1]
    acc = jnp.zeros((RANK, cols), jnp.float32)
    for kz in range(4):
        for ref, c in ((pa_ref, core), (pb_ref, 1 - core)):
            block = ((zh - kz + 4) % 4) * 2 + c
            rows = pl.ds(pl.multiple_of(block * ROWS, ROWS), ROWS)
            grads = jnp.concatenate(
                [
                    gq1_ref[rows, :],
                    gq2_ref[rows, :],
                    gk_ref[rows, :].astype(jnp.bfloat16),
                    gv_ref[rows, :].astype(jnp.bfloat16),
                ],
                axis=1,
            )
            acc += dot(ref[kz], grads, TN)
    out_ref[...] = acc.astype(jnp.bfloat16)


def outer(where, pa, pb, gq1, gq2, gk, gv):
    cols = gq1.shape[1] + gq2.shape[1] + 2 * HEAD
    return pl.pallas_call(
        outer_body,
        in_specs=[SMEM] + [pl.BlockSpec(memory_space=pltpu.VMEM)] * 6,
        out_specs=pl.BlockSpec(memory_space=pltpu.VMEM),
        out_shape=jax.ShapeDtypeStruct((RANK, cols), jnp.bfloat16),
        name="outer",
    )(where, pa, pb, gq1, gq2, gk, gv)


def turned(size, by):
    return [(i, (i + by) % size) for i in range(size)]


def core_swap(x):
    return lax.ppermute(x, "c", [(0, 1), (1, 0)])


def on_device(hidden_in, queries, keys, values, out_grad, doc_ids, flora_proj):
    core = lax.axis_index("c")
    zh = lax.axis_index("zh")
    x = lax.axis_index("x")
    y = lax.axis_index("y")
    where = jnp.stack([core, zh, x, y]).astype(jnp.int32)

    rows = lax.dynamic_slice_in_dim(flora_proj, y * ROWS, ROWS, 0)
    rows = lax.ppermute(
        rows, ("x", "zh"), [(a * 4 + b, b * 4 + a) for a in range(4) for b in range(4)]
    )
    along_x = [rows] + [lax.ppermute(rows, "x", turned(4, k)) for k in range(1, 4)]
    piece = jnp.stack(along_x)
    pieces = [piece] * 8
    up = down = piece
    for k in range(1, 5):
        up = lax.ppermute(up, "y", turned(8, 1))
        pieces[k] = up
        if k < 4:
            down = lax.ppermute(down, "y", turned(8, -1))
            pieces[8 - k] = down

    halves = hidden_in.reshape(ROWS, 4, 2, 1024)
    theirs = core_swap(
        lax.dynamic_index_in_dim(halves, 1 - core, 2, keepdims=False).reshape(ROWS, 4096)
    )

    first, second = pack(queries, out_grad, keys, values, doc_ids)
    first = lax.all_to_all(first, ("zh", "c"), 0, 0, tiled=True)
    second = lax.all_to_all(second, ("zh", "c"), 0, 0, tiled=True)
    base = 2 * FIRST_HEADS * ROWS
    other = core_swap(first[:, base : base + ROWS, :])

    gq1, gk, gv = attention(FIRST_HEADS, where, first, first, other)

    own, back = project(where, hidden_in, theirs, pieces)
    projected = (own + core_swap(back)).astype(jnp.bfloat16)
    pa = jnp.stack(
        [projected] + [lax.ppermute(projected, "zh", turned(4, k)) for k in range(1, 4)]
    )
    pb = core_swap(pa)

    gq2, gk, gv = attention(HEADS - FIRST_HEADS, where, second, first, other, (gk, gv))
    local = outer(where, pa, pb, gq1, gq2, gk, gv)

    parts = lax.all_to_all(
        local.reshape(64, 4, local.shape[1]), ("x", "y", "zl"), 0, 0, tiled=True
    )
    sums = jnp.sum(parts.astype(jnp.float32), axis=0)
    flora_q = sums[:, : HEADS * HEAD]
    kv = sums[:, HEADS * HEAD :].reshape(4, 2, 8, 16).transpose(2, 0, 1, 3).reshape(8, 1, 128)
    kv = lax.all_to_all(kv, ("zh", "c"), 0, 0, tiled=True)
    kv = kv.reshape(4, 2, 4, 2, 16).sum(axis=1)
    kv = kv.transpose(2, 1, 3, 0).reshape(2, 4, 64)
    return (flora_q, kv[0], kv[1])


def solution(mesh):
    fine = Mesh(np.asarray(mesh.devices).reshape(4, 8, 2, 4, 2), ("x", "y", "zl", "zh", "c"))
    dp = ("x", "y", "zl")
    uly = ("zh", "c")
    placed = (P(dp, uly, None),) * 5 + (P(dp, uly), P(uly, None))
    return jax.shard_map(
        on_device,
        mesh=fine,
        in_specs=placed,
        out_specs=(P(dp, uly), P(dp, uly), P(dp, uly)),
        check_vma=False,
    )
```

```python
import math

import jax
import jax.numpy as jnp
import numpy as np
from jax import lax
from jax.experimental import pallas as pl
from jax.experimental.pallas import tpu as pltpu
from jax.sharding import Mesh
from jax.sharding import PartitionSpec as P


HEAD = 128
ROWS = 128
RANK = 256
SEQ = 1024
BLOCKS = SEQ // ROWS
BAND = 640
INV_ROOT = 1.0 / math.sqrt(HEAD)
EXP2_SCALE = INV_ROOT * math.log2(math.e)
FIRST_HEADS = 3
HEADS = 4
TAIL = 16

NT = (((1,), (1,)), ((), ()))
TN = (((0,), (0,)), ((), ()))
NN = (((1,), (0,)), ((), ()))


def dot(a, b, dims):
    return lax.dot_general(a, b, dims, preferred_element_type=jnp.float32)


def full(shape):
    return pl.BlockSpec(shape, lambda *_: (0,) * len(shape))


SMEM = pl.BlockSpec(memory_space=pltpu.SMEM)


def pack_body(q_ref, g_ref, k_ref, v_ref, ids_ref, first_ref, second_ref):
    peer = pl.program_id(0)
    n1, n2 = FIRST_HEADS, HEADS - FIRST_HEADS
    for h in range(n1):
        cols = slice(h * HEAD, (h + 1) * HEAD)
        first_ref[0, h * ROWS : (h + 1) * ROWS, :] = q_ref[0, :, cols]
        first_ref[0, (n1 + h) * ROWS : (n1 + h + 1) * ROWS, :] = g_ref[0, :, cols]
    base = 2 * n1 * ROWS
    first_ref[0, base : base + ROWS, :] = jnp.where(peer % 2 == 0, k_ref[0], v_ref[0])
    first_ref[0, base + ROWS : base + ROWS + TAIL, :] = jnp.broadcast_to(
        ids_ref[...].astype(jnp.float32), (TAIL, ROWS)
    ).astype(jnp.bfloat16)
    for h in range(n2):
        cols = slice((n1 + h) * HEAD, (n1 + h + 1) * HEAD)
        second_ref[0, h * ROWS : (h + 1) * ROWS, :] = q_ref[0, :, cols]
        second_ref[0, (n2 + h) * ROWS : (n2 + h + 1) * ROWS, :] = g_ref[0, :, cols]


def pack(queries, out_grad, keys, values, ids):
    r1 = 2 * FIRST_HEADS * ROWS + ROWS + TAIL
    r2 = 2 * (HEADS - FIRST_HEADS) * ROWS
    wide = pl.BlockSpec((1, ROWS, HEADS * HEAD), lambda u: (0, 0, u))
    thin = pl.BlockSpec((1, ROWS, HEAD), lambda u: (0, 0, u // 2))
    return pl.pallas_call(
        pack_body,
        grid=(8,),
        in_specs=[wide, wide, thin, thin, full((1, ROWS))],
        out_specs=[
            pl.BlockSpec((1, r1, HEAD), lambda u: (u, 0, 0)),
            pl.BlockSpec((1, r2, HEAD), lambda u: (u, 0, 0)),
        ],
        out_shape=[
            jax.ShapeDtypeStruct((8, r1, HEAD), jnp.bfloat16),
            jax.ShapeDtypeStruct((8, r2, HEAD), jnp.bfloat16),
        ],
        name="pack",
    )(queries, out_grad, keys, values, ids)


def attention_body(heads, first, where_ref, qg_ref, kv_ref, other_ref, *rest):
    if first:
        gq_ref, gk_ref, gv_ref, k_sc, v_sc, starts = rest
    else:
        gk_in, gv_in, gq_ref, gk_ref, gv_ref, k_sc, v_sc, starts = rest
    i = pl.program_id(0)
    m_cols = heads * ROWS
    base = 2 * FIRST_HEADS * ROWS
    core = where_ref[0]

    @pl.when(i == 0)
    def _():
        if first:
            gk_ref[...] = jnp.zeros_like(gk_ref)
            gv_ref[...] = jnp.zeros_like(gv_ref)
        else:
            gk_ref[...] = gk_in[...]
            gv_ref[...] = gv_in[...]

        @pl.when(core == 0)
        def _():
            for b in range(BLOCKS):
                k_sc[b * ROWS : (b + 1) * ROWS, :] = kv_ref[b, base : base + ROWS, :]
                v_sc[b * ROWS : (b + 1) * ROWS, :] = other_ref[b]

        @pl.when(core != 0)
        def _():
            for b in range(BLOCKS):
                v_sc[b * ROWS : (b + 1) * ROWS, :] = kv_ref[b, base : base + ROWS, :]
                k_sc[b * ROWS : (b + 1) * ROWS, :] = other_ref[b]

        count0 = jnp.zeros((1, ROWS), jnp.float32)
        count1 = jnp.zeros((1, ROWS), jnp.float32)
        for b in range(BLOCKS):
            ids_b = kv_ref[b, base + ROWS : base + ROWS + TAIL, :].astype(jnp.float32)[:1]
            count0 += jnp.where(ids_b < 0.5, 1.0, 0.0)
            count1 += jnp.where(ids_b < 1.5, 1.0, 0.0)
        starts[0] = jnp.sum(count0).astype(jnp.int32)
        starts[1] = jnp.sum(count1).astype(jnp.int32)

    start1, start2 = starts[0], starts[1]

    def start_of(pos):
        return jnp.where(pos < start1, 0, jnp.where(pos < start2, start1, start2))

    first_block = start_of(i * ROWS) // ROWS
    blocks = jnp.minimum(i - first_block + 1, BAND // ROWS)

    def step(count):
        keys = count * ROWS
        q_pos = i * ROWS + lax.broadcasted_iota(jnp.int32, (1, ROWS), 1)
        q_pos = jnp.concatenate([q_pos] * heads, axis=1)
        q_start = start_of(q_pos)
        key_start = pl.multiple_of((i - (count - 1)) * ROWS, ROWS)
        band = pl.ds(key_start, keys)
        k = k_sc[band, :]
        v = v_sc[band, :]
        q = qg_ref[i, : heads * ROWS, :]
        g = qg_ref[i, heads * ROWS : 2 * heads * ROWS, :]
        k_pos = key_start + lax.broadcasted_iota(jnp.int32, (keys, m_cols), 0)
        scores = dot(k, q, NT) * EXP2_SCALE
        allowed = (k_pos <= q_pos) & (k_pos >= q_start)
        scores = jnp.where(allowed, scores, -jnp.inf)
        peak = jnp.max(scores, axis=0, keepdims=True)
        weights = jnp.exp2(scores - peak)
        inv = 1.0 / jnp.sum(weights, axis=0, keepdims=True)
        grad_probs = dot(v, g, NT)
        probs = weights * inv
        delta = jnp.sum(probs * grad_probs, axis=0, keepdims=True)
        probs_low = probs.astype(jnp.bfloat16)
        grad_scores = (probs * (grad_probs - delta)).astype(jnp.bfloat16)
        gv_ref[band, :] += dot(probs_low, g, NN)
        gk_ref[band, :] += dot(grad_scores, q, NN) * INV_ROOT
        gq = (dot(k, grad_scores, TN) * INV_ROOT).astype(jnp.bfloat16)
        for h in range(heads):
            gq_ref[:, h * HEAD : (h + 1) * HEAD] = gq[:, h * ROWS : (h + 1) * ROWS].T

    for count in range(1, BAND // ROWS + 1):
        pl.when(blocks == count)(lambda count=count: step(count))


def attention(heads, where, qg, kv, other, so_far=None):
    first = so_far is None
    so_far = () if first else tuple(so_far)
    wide = (SEQ, HEAD)
    return pl.pallas_call(
        lambda *refs: attention_body(heads, first, *refs),
        grid=(BLOCKS,),
        in_specs=[SMEM, full(qg.shape), full(kv.shape), full(other.shape)]
        + [full(wide)] * len(so_far),
        out_specs=[
            pl.BlockSpec((ROWS, heads * HEAD), lambda i: (i, 0)),
            full(wide),
            full(wide),
        ],
        out_shape=[
            jax.ShapeDtypeStruct((SEQ, heads * HEAD), jnp.bfloat16),
            jax.ShapeDtypeStruct(wide, jnp.float32),
            jax.ShapeDtypeStruct(wide, jnp.float32),
        ],
        scratch_shapes=[
            pltpu.VMEM(wide, jnp.bfloat16),
            pltpu.VMEM(wide, jnp.bfloat16),
            pltpu.SMEM((2,), jnp.int32),
        ],
        name="attention_first" if first else "attention_rest",
    )(where, qg, kv, other, *so_far)


def pick(where, hidden):
    def body(where_ref, h_ref, out_ref):
        out_ref[...] = h_ref[0]

    return pl.pallas_call(
        body,
        grid_spec=pltpu.PrefetchScalarGridSpec(
            num_scalar_prefetch=1,
            grid=(4,),
            in_specs=[pl.BlockSpec((1, ROWS, 1024), lambda b, w: (0, 0, 2 * b + 1 - w[0]))],
            out_specs=pl.BlockSpec((ROWS, 1024), lambda b, w: (0, b)),
        ),
        out_shape=jax.ShapeDtypeStruct((ROWS, 4096), jnp.bfloat16),
        name="pick",
    )(where, hidden)


def kernel(body, where, arrays, out_shape, name):
    many = isinstance(out_shape, list)
    vmem = pl.BlockSpec(memory_space=pltpu.VMEM)
    return pl.pallas_call(
        body,
        in_specs=[SMEM] + [vmem] * len(arrays),
        out_specs=[vmem] * len(out_shape) if many else vmem,
        out_shape=out_shape,
        name=name,
    )(where, *arrays)


def assemble_body(where_ref, *refs):
    out_ref = refs[8]
    y = where_ref[3]
    for k in range(8):
        row = (y - k + 8) % 8
        out_ref[pl.ds(pl.multiple_of(row * ROWS, ROWS), ROWS), :] = refs[k][...]


def project_body(where_ref, mine_ref, theirs_ref, *rest):
    pieces, (own_ref, back_ref) = rest[:4], rest[4:]
    core, x = where_ref[0], where_ref[2]
    own = jnp.zeros((ROWS, RANK), jnp.float32)
    back = jnp.zeros((ROWS, RANK), jnp.float32)
    for kx in range(4):
        part = (x - kx + 4) % 4
        w = pieces[kx][...]
        at = pl.multiple_of((part * 2 + core) * 1024, 1024)
        own += dot(mine_ref[0, :, pl.ds(at, 1024)], w, NN)
        at = pl.multiple_of(part * 1024, 1024)
        back += dot(theirs_ref[:, pl.ds(at, 1024)], w, NN)
    own_ref[...] = own
    back_ref[...] = back


def turn_body(where_ref, p0, p1, p2, p3, pb_ref, out_ref):
    core, zh = where_ref[0], where_ref[1]
    for kz, own in enumerate((p0, p1, p2, p3)):
        for piece, c in ((own[...], core), (pb_ref[kz], 1 - core)):
            block = ((zh - kz + 4) % 4) * 2 + c
            out_ref[:, pl.ds(pl.multiple_of(block * ROWS, ROWS), ROWS)] = piece.T


def outer_first_body(where_ref, pt_ref, gq_ref, out_ref):
    out_ref[...] = dot(pt_ref[...], gq_ref[...], NN).astype(jnp.bfloat16)


def outer_rest_body(where_ref, pt_ref, gq_ref, gk_ref, gv_ref, q_ref, keep_ref, send_ref):
    core = where_ref[0]
    grads = jnp.concatenate(
        [gq_ref[...], gk_ref[...].astype(jnp.bfloat16), gv_ref[...].astype(jnp.bfloat16)],
        axis=1,
    )
    sums = dot(pt_ref[...], grads, NN)
    q_ref[...] = sums[:, :HEAD].astype(jnp.bfloat16)
    turned_k = sums[:, HEAD : 2 * HEAD].T
    turned_v = sums[:, 2 * HEAD :].T
    for u in range(8):
        block = jnp.concatenate(
            [turned_k[u * 16 : (u + 1) * 16], turned_v[u * 16 : (u + 1) * 16]], axis=0
        )

        @pl.when(core == u % 2)
        def _():
            keep_ref[u // 2] = block

        @pl.when(core != u % 2)
        def _():
            send_ref[u // 2] = block.astype(jnp.bfloat16)


def add_body(where_ref, keep_ref, got_ref, own_ref, o1_ref, o2_ref, o3_ref):
    zh = where_ref[1]
    for k, ref in enumerate((own_ref, o1_ref, o2_ref, o3_ref)):
        to = (zh + k) % 4
        ref[...] = (keep_ref[to] + got_ref[to].astype(jnp.float32)).astype(jnp.bfloat16)


def mix_body(where_ref, q_ref, p0, p1, p2, p3, out_ref, sc):
    zh = where_ref[1]
    for k, ref in enumerate((p0, p1, p2, p3)):
        head = (zh - k + 4) % 4
        sc[head] = ref[...].astype(jnp.float32)
    stacked = sc[...].reshape(128, RANK).astype(jnp.bfloat16)
    row = lax.broadcasted_iota(jnp.int32, (128, 128), 0)
    col = lax.broadcasted_iota(jnp.int32, (128, 128), 1)
    head, side, c = row // 32, (row // 16) % 2, row % 16
    order = jnp.where(col == side * 64 + c * 4 + head, 1.0, 0.0).astype(jnp.bfloat16)
    out_ref[:, :HEAD] = q_ref[...]
    out_ref[:, HEAD:] = dot(stacked, order, TN).astype(jnp.bfloat16)


def turned(size, by):
    return [(i, (i + by) % size) for i in range(size)]


def core_swap(x):
    return lax.ppermute(x, "c", [(0, 1), (1, 0)])


def on_device(hidden_in, queries, keys, values, out_grad, doc_ids, flora_proj):
    core = lax.axis_index("c")
    zh = lax.axis_index("zh")
    x = lax.axis_index("x")
    y = lax.axis_index("y")
    where = jnp.stack([core, zh, x, y]).astype(jnp.int32)

    rows = lax.dynamic_slice_in_dim(flora_proj, y * ROWS, ROWS, 0)
    rows = lax.ppermute(
        rows, ("x", "zh"), [(a * 4 + b, b * 4 + a) for a in range(4) for b in range(4)]
    )
    first, second = pack(queries, out_grad, keys, values, doc_ids)
    rows, first = lax.optimization_barrier((rows, first))
    first = lax.all_to_all(first, ("zh", "c"), 0, 0, tiled=True)

    along_y = [rows] + [lax.ppermute(rows, "y", turned(8, k)) for k in (1, 7, 2, 6, 3, 5, 4)]
    along_y = [along_y[(0, 1, 3, 5, 7, 6, 4, 2)[k]] for k in range(8)]
    block = kernel(
        assemble_body, where, along_y, jax.ShapeDtypeStruct((1024, RANK), jnp.bfloat16), "assemble"
    )
    pieces = [block] + [lax.ppermute(block, "x", turned(4, k)) for k in range(1, 4)]
    where_later, block = lax.optimization_barrier((where, block))
    theirs = core_swap(pick(where_later, hidden_in))

    base = 2 * FIRST_HEADS * ROWS
    other = core_swap(first[:, base : base + ROWS, :])
    second = lax.all_to_all(second, ("zh", "c"), 0, 0, tiled=True)

    half = jax.ShapeDtypeStruct((ROWS, RANK), jnp.float32)
    own, back = kernel(
        project_body, where, [hidden_in, theirs, *pieces], [half, half], "project"
    )
    projected = (own + core_swap(back)).astype(jnp.bfloat16)
    along_z = [projected] + [lax.ppermute(projected, "zh", turned(4, k)) for k in range(1, 4)]
    gq, gk, gv = attention(FIRST_HEADS, where, first, first, other)
    *along_z, gq = lax.optimization_barrier((*along_z, gq))
    pb = core_swap(jnp.stack(along_z))
    pt = kernel(
        turn_body, where, [*along_z, pb], jax.ShapeDtypeStruct((RANK, SEQ), jnp.bfloat16), "turn"
    )

    early = kernel(
        outer_first_body,
        where,
        [pt, gq],
        jax.ShapeDtypeStruct((RANK, FIRST_HEADS * HEAD), jnp.bfloat16),
        "outer_first",
    )

    def reduced(local):
        parts = local.reshape(64, 4, local.shape[1])
        parts = lax.all_to_all(parts, ("x", "y", "zl"), 0, 0, tiled=True)
        return jnp.sum(parts.astype(jnp.float32), axis=0)

    early, second = lax.optimization_barrier((early, second))
    early = reduced(early)
    gq, gk, gv = attention(HEADS - FIRST_HEADS, where, second, first, other, (gk, gv))
    q_last, keep, send = kernel(
        outer_rest_body,
        where,
        [pt, gq, gk, gv],
        [
            jax.ShapeDtypeStruct((RANK, HEAD), jnp.bfloat16),
            jax.ShapeDtypeStruct((4, 32, RANK), jnp.float32),
            jax.ShapeDtypeStruct((4, 32, RANK), jnp.bfloat16),
        ],
        "outer_rest",
    )
    tile = jax.ShapeDtypeStruct((32, RANK), jnp.bfloat16)
    tiles = kernel(add_body, where, [keep, core_swap(send)], [tile] * 4, "add")
    tiles = [tiles[0]] + [lax.ppermute(tiles[k], "zh", turned(4, k)) for k in range(1, 4)]
    late = pl.pallas_call(
        mix_body,
        in_specs=[SMEM] + [pl.BlockSpec(memory_space=pltpu.VMEM)] * 5,
        out_specs=pl.BlockSpec(memory_space=pltpu.VMEM),
        out_shape=jax.ShapeDtypeStruct((RANK, 2 * HEAD), jnp.bfloat16),
        scratch_shapes=[pltpu.VMEM((4, 32, RANK), jnp.float32)],
        name="mix",
    )(where, q_last, *tiles)
    early, late = lax.optimization_barrier((early, late))
    late = reduced(late)
    return (
        jnp.concatenate([early, late[:, :HEAD]], axis=1),
        late[:, HEAD : HEAD + 64],
        late[:, HEAD + 64 :],
    )


def solution(mesh):
    fine = Mesh(np.asarray(mesh.devices).reshape(4, 8, 2, 4, 2), ("x", "y", "zl", "zh", "c"))
    dp = ("x", "y", "zl")
    uly = ("zh", "c")
    placed = (P(dp, uly, None),) * 5 + (P(dp, uly), P(uly, None))
    return jax.shard_map(
        on_device,
        mesh=fine,
        in_specs=placed,
        out_specs=(P(dp, uly), P(dp, uly), P(dp, uly)),
        check_vma=False,
    )
```

```python
import math

import jax
import jax.numpy as jnp
import numpy as np
from jax import lax
from jax.experimental import pallas as pl
from jax.experimental.pallas import tpu as pltpu
from jax.sharding import Mesh
from jax.sharding import PartitionSpec as P


HEAD = 128
ROWS = 128
RANK = 256
SEQ = 1024
BLOCKS = SEQ // ROWS
BAND = 640
INV_ROOT = 1.0 / math.sqrt(HEAD)
EXP2_SCALE = INV_ROOT * math.log2(math.e)
HEADS = 4
TAIL = 16
KV_AT = 2 * HEADS * ROWS

NT = (((1,), (1,)), ((), ()))
TN = (((0,), (0,)), ((), ()))
NN = (((1,), (0,)), ((), ()))


def dot(a, b, dims):
    return lax.dot_general(a, b, dims, preferred_element_type=jnp.float32)


def full(shape):
    return pl.BlockSpec(shape, lambda *_: (0,) * len(shape))


SMEM = pl.BlockSpec(memory_space=pltpu.SMEM)


def pack_body(q_ref, g_ref, k_ref, v_ref, ids_ref, out_ref):
    for p in range(2):
        for h in range(HEADS):
            cols = slice((p * HEADS + h) * HEAD, (p * HEADS + h + 1) * HEAD)
            out_ref[p, h * ROWS : (h + 1) * ROWS, :] = q_ref[0, :, cols]
            out_ref[p, (HEADS + h) * ROWS : (HEADS + h + 1) * ROWS, :] = g_ref[0, :, cols]
        out_ref[p, KV_AT : KV_AT + ROWS, :] = (v_ref if p else k_ref)[0]
        out_ref[p, KV_AT + ROWS :, :] = jnp.broadcast_to(
            ids_ref[...].astype(jnp.float32), (TAIL, ROWS)
        ).astype(jnp.bfloat16)


def pack(queries, out_grad, keys, values, ids):
    wide = pl.BlockSpec((1, ROWS, 2 * HEADS * HEAD), lambda u: (0, 0, u))
    thin = pl.BlockSpec((1, ROWS, HEAD), lambda u: (0, 0, u))
    return pl.pallas_call(
        pack_body,
        grid=(4,),
        in_specs=[wide, wide, thin, thin, full((1, ROWS))],
        out_specs=pl.BlockSpec((2, KV_AT + ROWS + TAIL, HEAD), lambda u: (u, 0, 0)),
        out_shape=jax.ShapeDtypeStruct((8, KV_AT + ROWS + TAIL, HEAD), jnp.bfloat16),
        name="pack",
    )(queries, out_grad, keys, values, ids)


def attention_body(
    where_ref, all_ref, other_ref, gq_ref, gk_ref, gv_ref, k_sc, v_sc, starts
):
    heads = HEADS
    i = pl.program_id(0)
    m_cols = heads * ROWS
    base = KV_AT
    core = where_ref[0]

    @pl.when(i == 0)
    def _():
        gk_ref[...] = jnp.zeros_like(gk_ref)
        gv_ref[...] = jnp.zeros_like(gv_ref)

        @pl.when(core == 0)
        def _():
            for b in range(BLOCKS):
                k_sc[b * ROWS : (b + 1) * ROWS, :] = all_ref[b, base : base + ROWS, :]
                v_sc[b * ROWS : (b + 1) * ROWS, :] = other_ref[b]

        @pl.when(core != 0)
        def _():
            for b in range(BLOCKS):
                v_sc[b * ROWS : (b + 1) * ROWS, :] = all_ref[b, base : base + ROWS, :]
                k_sc[b * ROWS : (b + 1) * ROWS, :] = other_ref[b]

        count0 = jnp.zeros((1, ROWS), jnp.float32)
        count1 = jnp.zeros((1, ROWS), jnp.float32)
        for b in range(BLOCKS):
            ids_b = all_ref[b, base + ROWS : base + ROWS + TAIL, :].astype(jnp.float32)[:1]
            count0 += jnp.where(ids_b < 0.5, 1.0, 0.0)
            count1 += jnp.where(ids_b < 1.5, 1.0, 0.0)
        starts[0] = jnp.sum(count0).astype(jnp.int32)
        starts[1] = jnp.sum(count1).astype(jnp.int32)

    start1, start2 = starts[0], starts[1]

    def start_of(pos):
        return jnp.where(pos < start1, 0, jnp.where(pos < start2, start1, start2))

    first_block = start_of(i * ROWS) // ROWS
    blocks = jnp.minimum(i - first_block + 1, BAND // ROWS)

    def step(count):
        keys = count * ROWS
        q_pos = i * ROWS + lax.broadcasted_iota(jnp.int32, (1, ROWS), 1)
        q_pos = jnp.concatenate([q_pos] * heads, axis=1)
        q_start = start_of(q_pos)
        key_start = pl.multiple_of((i - (count - 1)) * ROWS, ROWS)
        band = pl.ds(key_start, keys)
        k = k_sc[band, :]
        v = v_sc[band, :]
        q = all_ref[i, : heads * ROWS, :]
        g = all_ref[i, heads * ROWS : 2 * heads * ROWS, :]
        k_pos = key_start + lax.broadcasted_iota(jnp.int32, (keys, m_cols), 0)
        scores = dot(k, q, NT) * EXP2_SCALE
        allowed = (k_pos <= q_pos) & (k_pos >= q_start)
        scores = jnp.where(allowed, scores, -jnp.inf)
        peak = jnp.max(scores, axis=0, keepdims=True)
        weights = jnp.exp2(scores - peak)
        inv = 1.0 / jnp.sum(weights, axis=0, keepdims=True)
        grad_probs = dot(v, g, NT)
        probs = weights * inv
        delta = jnp.sum(probs * grad_probs, axis=0, keepdims=True)
        probs_low = probs.astype(jnp.bfloat16)
        grad_scores = (probs * (grad_probs - delta)).astype(jnp.bfloat16)
        gv_ref[band, :] += dot(probs_low, g, NN)
        gk_ref[band, :] += dot(grad_scores, q, NN) * INV_ROOT
        gq = (dot(k, grad_scores, TN) * INV_ROOT).astype(jnp.bfloat16)
        for h in range(heads):
            gq_ref[:, h * HEAD : (h + 1) * HEAD] = gq[:, h * ROWS : (h + 1) * ROWS].T

    for count in range(1, BAND // ROWS + 1):
        pl.when(blocks == count)(lambda count=count: step(count))


def attention(where, everything, other):
    wide = (SEQ, HEAD)
    return pl.pallas_call(
        attention_body,
        grid=(BLOCKS,),
        in_specs=[SMEM, full(everything.shape), full(other.shape)],
        out_specs=[
            pl.BlockSpec((ROWS, HEADS * HEAD), lambda i: (i, 0)),
            full(wide),
            full(wide),
        ],
        out_shape=[
            jax.ShapeDtypeStruct((SEQ, HEADS * HEAD), jnp.bfloat16),
            jax.ShapeDtypeStruct(wide, jnp.float32),
            jax.ShapeDtypeStruct(wide, jnp.float32),
        ],
        scratch_shapes=[
            pltpu.VMEM(wide, jnp.bfloat16),
            pltpu.VMEM(wide, jnp.bfloat16),
            pltpu.SMEM((2,), jnp.int32),
        ],
        name="attention",
    )(where, everything, other)


def pick(where, hidden):
    def body(where_ref, h_ref, out_ref):
        out_ref[...] = h_ref[0]

    return pl.pallas_call(
        body,
        grid_spec=pltpu.PrefetchScalarGridSpec(
            num_scalar_prefetch=1,
            grid=(4,),
            in_specs=[pl.BlockSpec((1, ROWS, 1024), lambda b, w: (0, 0, 2 * b + 1 - w[0]))],
            out_specs=pl.BlockSpec((ROWS, 1024), lambda b, w: (0, b)),
        ),
        out_shape=jax.ShapeDtypeStruct((ROWS, 4096), jnp.bfloat16),
        name="pick",
    )(where, hidden)


def kernel(body, where, arrays, out_shape, name):
    many = isinstance(out_shape, list)
    vmem = pl.BlockSpec(memory_space=pltpu.VMEM)
    scalars = () if where is None else (where,)
    return pl.pallas_call(
        body,
        in_specs=[SMEM] * len(scalars) + [vmem] * len(arrays),
        out_specs=[vmem] * len(out_shape) if many else vmem,
        out_shape=out_shape,
        name=name,
    )(*scalars, *arrays)


def assemble_body(where_ref, near_ref, far_ref, out_ref):
    y = where_ref[3]
    for k in range(2):
        for half, ref in enumerate((near_ref, far_ref)):
            row = (y % 4) ^ (2 * k) ^ half
            out_ref[pl.ds(pl.multiple_of(row * 256, 256), 256), :] = ref[k]


def project_body(where_ref, mine_ref, theirs_ref, *rest):
    pieces, (own_ref, back_ref) = rest[:4], rest[4:]
    core, x = where_ref[0], where_ref[2]
    own = jnp.zeros((ROWS, RANK), jnp.float32)
    back = jnp.zeros((ROWS, RANK), jnp.float32)
    for kx in range(4):
        part = (x - kx + 4) % 4
        w = pieces[kx][...]
        at = pl.multiple_of((part * 2 + core) * 1024, 1024)
        own += dot(mine_ref[0, :, pl.ds(at, 1024)], w, NN)
        at = pl.multiple_of(part * 1024, 1024)
        back += dot(theirs_ref[:, pl.ds(at, 1024)], w, NN)
    own_ref[...] = own
    back_ref[...] = back


def outer_body(p_ref, gq_ref, gk_ref, gv_ref, q_ref, send_ref):
    turned_p = p_ref[...].reshape(SEQ, RANK).T
    grads = jnp.concatenate(
        [gq_ref[...], gk_ref[...].astype(jnp.bfloat16), gv_ref[...].astype(jnp.bfloat16)],
        axis=1,
    )
    sums = dot(turned_p, grads, NN)
    q_ref[...] = sums[:, : HEADS * HEAD].astype(jnp.bfloat16)
    turned_k = sums[:, HEADS * HEAD : HEADS * HEAD + HEAD].T.astype(jnp.bfloat16)
    turned_v = sums[:, HEADS * HEAD + HEAD :].T.astype(jnp.bfloat16)
    for u in range(8):
        send_ref[u, :16] = turned_k[u * 16 : (u + 1) * 16]
        send_ref[u, 16:] = turned_v[u * 16 : (u + 1) * 16]


def mix_body(q_ref, kv_ref, out_ref):
    sums = [
        kv_ref[2 * g].astype(jnp.float32) + kv_ref[2 * g + 1].astype(jnp.float32)
        for g in range(4)
    ]
    stacked = jnp.concatenate(sums, axis=0).astype(jnp.bfloat16)
    row = lax.broadcasted_iota(jnp.int32, (128, 128), 0)
    col = lax.broadcasted_iota(jnp.int32, (128, 128), 1)
    head, side, c = row // 32, (row // 16) % 2, row % 16
    order = jnp.where(col == side * 64 + c * 4 + head, 1.0, 0.0).astype(jnp.bfloat16)
    out_ref[:, : HEADS * HEAD] = q_ref[...]
    out_ref[:, HEADS * HEAD :] = dot(stacked, order, TN).astype(jnp.bfloat16)


def turned(size, by):
    return [(i, (i + by) % size) for i in range(size)]


def core_swap(x):
    return lax.ppermute(x, "c", [(0, 1), (1, 0)])


def on_device(hidden_in, queries, keys, values, out_grad, doc_ids, flora_proj):
    core = lax.axis_index("c")
    zh = lax.axis_index("zh")
    x = lax.axis_index("x")
    y = lax.axis_index("y")
    where = jnp.stack([core, zh, x, y]).astype(jnp.int32)
    low = jnp.bfloat16

    rows = lax.dynamic_slice_in_dim(flora_proj, (y % 4) * 256, 256, 0)
    rows = lax.ppermute(
        rows, ("x", "zh"), [(a * 4 + b, b * 4 + a) for a in range(4) for b in range(4)]
    )
    sent = pack(queries, out_grad, keys, values, doc_ids)
    rows, sent = lax.optimization_barrier((rows, sent))
    everything = lax.all_to_all(sent, ("zh", "c"), 0, 0, tiled=True)

    near = jnp.stack([rows, lax.ppermute(rows, "y", [(i, i ^ 2) for i in range(8)])])
    far = lax.ppermute(near, "y", [(i, i ^ 1) for i in range(8)])
    theirs = core_swap(pick(where, hidden_in))
    block = kernel(
        assemble_body, where, [near, far], jax.ShapeDtypeStruct((1024, RANK), low), "assemble"
    )
    pieces = [block] + [lax.ppermute(block, "x", turned(4, k)) for k in range(1, 4)]

    half = jax.ShapeDtypeStruct((ROWS, RANK), jnp.float32)
    own, back = kernel(
        project_body, where, [hidden_in, theirs, *pieces], [half, half], "project"
    )
    projected = (own + core_swap(back)).astype(low)
    other = core_swap(everything[:, KV_AT : KV_AT + ROWS, :])
    all_projected = lax.all_to_all(
        jnp.broadcast_to(projected, (8, ROWS, RANK)), ("zh", "c"), 0, 0, tiled=True
    )
    where, _ = lax.optimization_barrier((where, projected))
    gq, gk, gv = attention(where, everything, other)
    q_part, kv_part = kernel(
        outer_body,
        None,
        [all_projected, gq, gk, gv],
        [
            jax.ShapeDtypeStruct((RANK, HEADS * HEAD), low),
            jax.ShapeDtypeStruct((8, 32, RANK), low),
        ],
        "outer",
    )
    kv_part = lax.all_to_all(kv_part, ("zh", "c"), 0, 0, tiled=True)
    local = kernel(
        mix_body,
        None,
        [q_part, kv_part],
        jax.ShapeDtypeStruct((RANK, HEADS * HEAD + HEAD), low),
        "mix",
    )
    parts = local.reshape(64, 4, local.shape[1])
    parts = lax.all_to_all(parts, ("x", "y", "zl"), 0, 0, tiled=True)
    sums = jnp.sum(parts.astype(jnp.float32), axis=0)
    at = HEADS * HEAD
    return sums[:, :at], sums[:, at : at + 64], sums[:, at + 64 :]


def solution(mesh):
    fine = Mesh(np.asarray(mesh.devices).reshape(4, 8, 2, 4, 2), ("x", "y", "zl", "zh", "c"))
    dp = ("x", "y", "zl")
    uly = ("zh", "c")
    placed = (P(dp, uly, None),) * 5 + (P(dp, uly), P(uly, None))
    return jax.shard_map(
        on_device,
        mesh=fine,
        in_specs=placed,
        out_specs=(P(dp, uly), P(dp, uly), P(dp, uly)),
        check_vma=False,
    )
```

```python
import functools
import math

import jax
import jax.numpy as jnp
import numpy as np
from jax import lax
from jax.experimental import pallas as pl
from jax.experimental.pallas import tpu as pltpu
from jax.sharding import Mesh
from jax.sharding import PartitionSpec as P


HEAD = 128
ROWS = 128
RANK = 256
SEQ = 1024
BLOCKS = SEQ // ROWS
BAND = 640
INV_ROOT = 1.0 / math.sqrt(HEAD)
EXP2_SCALE = INV_ROOT * math.log2(math.e)
HEADS = 4
TAIL = 16
KV_AT = 2 * HEADS * ROWS

NT = (((1,), (1,)), ((), ()))
TN = (((0,), (0,)), ((), ()))
NN = (((1,), (0,)), ((), ()))


def dot(a, b, dims):
    return lax.dot_general(a, b, dims, preferred_element_type=jnp.float32)


def full(shape):
    return pl.BlockSpec(shape, lambda *_: (0,) * len(shape))


SMEM = pl.BlockSpec(memory_space=pltpu.SMEM)


def pack_body(q_ref, g_ref, k_ref, v_ref, ids_ref, out_ref):
    for p in range(2):
        for h in range(HEADS):
            cols = slice((p * HEADS + h) * HEAD, (p * HEADS + h + 1) * HEAD)
            out_ref[p, h * ROWS : (h + 1) * ROWS, :] = q_ref[0, :, cols]
            out_ref[p, (HEADS + h) * ROWS : (HEADS + h + 1) * ROWS, :] = g_ref[0, :, cols]
        out_ref[p, KV_AT : KV_AT + ROWS, :] = (v_ref if p else k_ref)[0]
        out_ref[p, KV_AT + ROWS :, :] = jnp.broadcast_to(
            ids_ref[...].astype(jnp.float32), (TAIL, ROWS)
        ).astype(jnp.bfloat16)


def pack(queries, out_grad, keys, values, ids):
    wide = pl.BlockSpec((1, ROWS, 2 * HEADS * HEAD), lambda u: (0, 0, u))
    thin = pl.BlockSpec((1, ROWS, HEAD), lambda u: (0, 0, u))
    return pl.pallas_call(
        pack_body,
        grid=(4,),
        in_specs=[wide, wide, thin, thin, full((1, ROWS))],
        out_specs=pl.BlockSpec((2, KV_AT + ROWS + TAIL, HEAD), lambda u: (u, 0, 0)),
        out_shape=jax.ShapeDtypeStruct((8, KV_AT + ROWS + TAIL, HEAD), jnp.bfloat16),
        name="pack",
    )(queries, out_grad, keys, values, ids)


def attention_body(
    where_ref, all_ref, other_ref, gq_ref, gk_ref, gv_ref, k_sc, v_sc, starts
):
    heads = HEADS
    i = pl.program_id(0)
    m_cols = heads * ROWS
    base = KV_AT
    core = where_ref[0]

    @pl.when(i == 0)
    def _():
        gk_ref[...] = jnp.zeros_like(gk_ref)
        gv_ref[...] = jnp.zeros_like(gv_ref)

        @pl.when(core == 0)
        def _():
            for b in range(BLOCKS):
                k_sc[b * ROWS : (b + 1) * ROWS, :] = all_ref[b, base : base + ROWS, :]
                v_sc[b * ROWS : (b + 1) * ROWS, :] = other_ref[b]

        @pl.when(core != 0)
        def _():
            for b in range(BLOCKS):
                v_sc[b * ROWS : (b + 1) * ROWS, :] = all_ref[b, base : base + ROWS, :]
                k_sc[b * ROWS : (b + 1) * ROWS, :] = other_ref[b]

        count0 = jnp.zeros((1, ROWS), jnp.float32)
        count1 = jnp.zeros((1, ROWS), jnp.float32)
        for b in range(BLOCKS):
            ids_b = all_ref[b, base + ROWS : base + ROWS + TAIL, :].astype(jnp.float32)[:1]
            count0 += jnp.where(ids_b < 0.5, 1.0, 0.0)
            count1 += jnp.where(ids_b < 1.5, 1.0, 0.0)
        starts[0] = jnp.sum(count0).astype(jnp.int32)
        starts[1] = jnp.sum(count1).astype(jnp.int32)

    start1, start2 = starts[0], starts[1]

    def start_of(pos):
        return jnp.where(pos < start1, 0, jnp.where(pos < start2, start1, start2))

    first_block = start_of(i * ROWS) // ROWS
    blocks = jnp.minimum(i - first_block + 1, BAND // ROWS)

    def step(count):
        keys = count * ROWS
        q_pos = i * ROWS + lax.broadcasted_iota(jnp.int32, (1, ROWS), 1)
        q_pos = jnp.concatenate([q_pos] * heads, axis=1)
        q_start = start_of(q_pos)
        key_start = pl.multiple_of((i - (count - 1)) * ROWS, ROWS)
        band = pl.ds(key_start, keys)
        k = k_sc[band, :]
        v = v_sc[band, :]
        q = all_ref[i, : heads * ROWS, :]
        g = all_ref[i, heads * ROWS : 2 * heads * ROWS, :]
        k_pos = key_start + lax.broadcasted_iota(jnp.int32, (keys, m_cols), 0)
        scores = dot(k, q, NT) * EXP2_SCALE
        allowed = (k_pos <= q_pos) & (k_pos >= q_start)
        scores = jnp.where(allowed, scores, -jnp.inf)
        peak = jnp.max(scores, axis=0, keepdims=True)
        weights = jnp.exp2(scores - peak)
        inv = 1.0 / jnp.sum(weights, axis=0, keepdims=True)
        grad_probs = dot(v, g, NT)
        probs = weights * inv
        delta = jnp.sum(probs * grad_probs, axis=0, keepdims=True)
        probs_low = probs.astype(jnp.bfloat16)
        grad_scores = (probs * (grad_probs - delta)).astype(jnp.bfloat16)
        gv_ref[band, :] += dot(probs_low, g, NN)
        gk_ref[band, :] += dot(grad_scores, q, NN) * INV_ROOT
        gq = (dot(k, grad_scores, TN) * INV_ROOT).astype(jnp.bfloat16)
        for h in range(heads):
            gq_ref[:, h * HEAD : (h + 1) * HEAD] = gq[:, h * ROWS : (h + 1) * ROWS].T

    for count in range(1, BAND // ROWS + 1):
        pl.when(blocks == count)(lambda count=count: step(count))


def attention(where, everything, other):
    wide = (SEQ, HEAD)
    return pl.pallas_call(
        attention_body,
        grid=(BLOCKS,),
        in_specs=[SMEM, full(everything.shape), full(other.shape)],
        out_specs=[
            pl.BlockSpec((ROWS, HEADS * HEAD), lambda i: (i, 0)),
            full(wide),
            full(wide),
        ],
        out_shape=[
            jax.ShapeDtypeStruct((SEQ, HEADS * HEAD), jnp.bfloat16),
            jax.ShapeDtypeStruct(wide, jnp.float32),
            jax.ShapeDtypeStruct(wide, jnp.float32),
        ],
        scratch_shapes=[
            pltpu.VMEM(wide, jnp.bfloat16),
            pltpu.VMEM(wide, jnp.bfloat16),
            pltpu.SMEM((2,), jnp.int32),
        ],
        name="attention",
    )(where, everything, other)


def pick(where, hidden):
    def body(where_ref, h_ref, out_ref):
        out_ref[...] = h_ref[0]

    return pl.pallas_call(
        body,
        grid_spec=pltpu.PrefetchScalarGridSpec(
            num_scalar_prefetch=1,
            grid=(4,),
            in_specs=[pl.BlockSpec((1, ROWS, 1024), lambda b, w: (0, 0, 2 * b + 1 - w[0]))],
            out_specs=pl.BlockSpec((ROWS, 1024), lambda b, w: (0, b)),
        ),
        out_shape=jax.ShapeDtypeStruct((ROWS, 4096), jnp.bfloat16),
        name="pick",
    )(where, hidden)


def kernel(body, where, arrays, out_shape, name):
    many = isinstance(out_shape, list)
    vmem = pl.BlockSpec(memory_space=pltpu.VMEM)
    scalars = () if where is None else (where,)
    return pl.pallas_call(
        body,
        in_specs=[SMEM] * len(scalars) + [vmem] * len(arrays),
        out_specs=[vmem] * len(out_shape) if many else vmem,
        out_shape=out_shape,
        name=name,
    )(*scalars, *arrays)


def project_body(half, where_ref, mine_ref, theirs_ref, *rest):
    pieces, (own_ref, back_ref) = rest[:4], rest[-2:]
    core, x, y = where_ref[0], where_ref[2], where_ref[3]
    if half:
        own, back = rest[4][...], rest[5][...]
    else:
        own = jnp.zeros((ROWS, RANK), jnp.float32)
        back = jnp.zeros((ROWS, RANK), jnp.float32)
    for kx in range(4):
        part = (x - kx + 4) % 4
        for k in range(2):
            row = (y % 4) ^ (2 * k) ^ half
            w = pieces[kx][k]
            at = pl.multiple_of((part * 2 + core) * 1024 + row * 256, 256)
            own += dot(mine_ref[0, :, pl.ds(at, 256)], w, NN)
            at = pl.multiple_of(part * 1024 + row * 256, 256)
            back += dot(theirs_ref[:, pl.ds(at, 256)], w, NN)
    own_ref[...] = own
    back_ref[...] = back


def outer_body(p_ref, gq_ref, gk_ref, gv_ref, q_ref, send_ref):
    turned_p = p_ref[...].reshape(SEQ, RANK).T
    grads = jnp.concatenate(
        [gq_ref[...], gk_ref[...].astype(jnp.bfloat16), gv_ref[...].astype(jnp.bfloat16)],
        axis=1,
    )
    sums = dot(turned_p, grads, NN)
    q_ref[...] = sums[:, : HEADS * HEAD].astype(jnp.bfloat16)
    turned_k = sums[:, HEADS * HEAD : HEADS * HEAD + HEAD].T.astype(jnp.bfloat16)
    turned_v = sums[:, HEADS * HEAD + HEAD :].T.astype(jnp.bfloat16)
    for u in range(8):
        send_ref[u, :16] = turned_k[u * 16 : (u + 1) * 16]
        send_ref[u, 16:] = turned_v[u * 16 : (u + 1) * 16]


def mix_body(q_ref, kv_ref, out_ref):
    sums = [
        kv_ref[2 * g].astype(jnp.float32) + kv_ref[2 * g + 1].astype(jnp.float32)
        for g in range(4)
    ]
    stacked = jnp.concatenate(sums, axis=0).astype(jnp.bfloat16)
    row = lax.broadcasted_iota(jnp.int32, (128, 128), 0)
    col = lax.broadcasted_iota(jnp.int32, (128, 128), 1)
    head, side, c = row // 32, (row // 16) % 2, row % 16
    order = jnp.where(col == side * 64 + c * 4 + head, 1.0, 0.0).astype(jnp.bfloat16)
    out_ref[:, : HEADS * HEAD] = q_ref[...]
    out_ref[:, HEADS * HEAD :] = dot(stacked, order, TN).astype(jnp.bfloat16)


def turned(size, by):
    return [(i, (i + by) % size) for i in range(size)]


def core_swap(x):
    return lax.ppermute(x, "c", [(0, 1), (1, 0)])


def on_device(hidden_in, queries, keys, values, out_grad, doc_ids, flora_proj):
    core = lax.axis_index("c")
    zh = lax.axis_index("zh")
    x = lax.axis_index("x")
    y = lax.axis_index("y")
    where = jnp.stack([core, zh, x, y]).astype(jnp.int32)
    low = jnp.bfloat16

    rows = lax.dynamic_slice_in_dim(flora_proj, (y % 4) * 256, 256, 0)
    rows = lax.ppermute(
        rows, ("x", "zh"), [(a * 4 + b, b * 4 + a) for a in range(4) for b in range(4)]
    )
    sent = pack(queries, out_grad, keys, values, doc_ids)
    picked = pick(where, hidden_in)
    rows, sent, picked = lax.optimization_barrier((rows, sent, picked))
    everything = lax.all_to_all(sent, ("zh", "c"), 0, 0, tiled=True)

    def spread(piece):
        return [piece] + [lax.ppermute(piece, "x", turned(4, k)) for k in (1, 3, 2)]

    theirs = core_swap(picked)
    near = jnp.stack([rows, lax.ppermute(rows, "y", [(i, i ^ 2) for i in range(8)])])
    far = lax.ppermute(near, "y", [(i, i ^ 1) for i in range(8)])
    half = [jax.ShapeDtypeStruct((ROWS, RANK), jnp.float32)] * 2
    sums = []
    for side, piece in enumerate((near, far)):
        one, back, three, two = (*spread(piece),)
        sums = kernel(
            functools.partial(project_body, side),
            where,
            [hidden_in, theirs, one, back, two, three, *sums],
            half,
            "project_far" if side else "project_near",
        )
    own, back = sums
    projected = (own + core_swap(back)).astype(low)
    other = core_swap(everything[:, KV_AT : KV_AT + ROWS, :])
    all_projected = lax.all_to_all(
        jnp.broadcast_to(projected, (8, ROWS, RANK)), ("zh", "c"), 0, 0, tiled=True
    )
    where, _ = lax.optimization_barrier((where, projected))
    gq, gk, gv = attention(where, everything, other)
    q_part, kv_part = kernel(
        outer_body,
        None,
        [all_projected, gq, gk, gv],
        [
            jax.ShapeDtypeStruct((RANK, HEADS * HEAD), low),
            jax.ShapeDtypeStruct((8, 32, RANK), low),
        ],
        "outer",
    )
    kv_part = lax.all_to_all(kv_part, ("zh", "c"), 0, 0, tiled=True)
    local = kernel(
        mix_body,
        None,
        [q_part, kv_part],
        jax.ShapeDtypeStruct((RANK, HEADS * HEAD + HEAD), low),
        "mix",
    )
    parts = local.reshape(64, 4, local.shape[1])
    parts = lax.all_to_all(parts, ("x", "y", "zl"), 0, 0, tiled=True)
    sums = jnp.sum(parts.astype(jnp.float32), axis=0)
    at = HEADS * HEAD
    return sums[:, :at], sums[:, at : at + 64], sums[:, at + 64 :]


def solution(mesh):
    fine = Mesh(np.asarray(mesh.devices).reshape(4, 8, 2, 4, 2), ("x", "y", "zl", "zh", "c"))
    dp = ("x", "y", "zl")
    uly = ("zh", "c")
    placed = (P(dp, uly, None),) * 5 + (P(dp, uly), P(uly, None))
    return jax.shard_map(
        on_device,
        mesh=fine,
        in_specs=placed,
        out_specs=(P(dp, uly), P(dp, uly), P(dp, uly)),
        check_vma=False,
    )
```

```python
import functools
import math

import jax
import jax.numpy as jnp
import numpy as np
from jax import lax
from jax.experimental import pallas as pl
from jax.experimental.pallas import tpu as pltpu
from jax.sharding import Mesh
from jax.sharding import PartitionSpec as P


HEAD = 128
ROWS = 128
RANK = 256
SEQ = 1024
BLOCKS = SEQ // ROWS
BAND = 640
INV_ROOT = 1.0 / math.sqrt(HEAD)
EXP2_SCALE = INV_ROOT * math.log2(math.e)
HEADS = 4
TAIL = 16
KV_AT = 2 * HEADS * ROWS
SMALL_VMEM = 16 * 2**20

NT = (((1,), (1,)), ((), ()))
TN = (((0,), (0,)), ((), ()))
NN = (((1,), (0,)), ((), ()))


def dot(a, b, dims):
    return lax.dot_general(a, b, dims, preferred_element_type=jnp.float32)


def full(shape):
    return pl.BlockSpec(shape, lambda *_: (0,) * len(shape))


SMEM = pl.BlockSpec(memory_space=pltpu.SMEM)


def pack_body(q_ref, g_ref, k_ref, v_ref, ids_ref, out_ref):
    for p in range(2):
        for h in range(HEADS):
            cols = slice((p * HEADS + h) * HEAD, (p * HEADS + h + 1) * HEAD)
            out_ref[p, h * ROWS : (h + 1) * ROWS, :] = q_ref[0, :, cols]
            out_ref[p, (HEADS + h) * ROWS : (HEADS + h + 1) * ROWS, :] = g_ref[0, :, cols]
        out_ref[p, KV_AT : KV_AT + ROWS, :] = (v_ref if p else k_ref)[0]
        out_ref[p, KV_AT + ROWS :, :] = jnp.broadcast_to(
            ids_ref[...].astype(jnp.float32), (TAIL, ROWS)
        ).astype(jnp.bfloat16)


def pack(queries, out_grad, keys, values, ids):
    wide = pl.BlockSpec((1, ROWS, 2 * HEADS * HEAD), lambda u: (0, 0, u))
    thin = pl.BlockSpec((1, ROWS, HEAD), lambda u: (0, 0, u))
    return pl.pallas_call(
        pack_body,
        grid=(4,),
        in_specs=[wide, wide, thin, thin, full((1, ROWS))],
        out_specs=pl.BlockSpec((2, KV_AT + ROWS + TAIL, HEAD), lambda u: (u, 0, 0)),
        out_shape=jax.ShapeDtypeStruct((8, KV_AT + ROWS + TAIL, HEAD), jnp.bfloat16),
        name="pack",
    )(queries, out_grad, keys, values, ids)


def attention_body(
    where_ref, all_ref, other_ref, gq_ref, gk_ref, gv_ref, k_sc, v_sc, starts
):
    heads = HEADS
    i = pl.program_id(0)
    m_cols = heads * ROWS
    base = KV_AT
    core = where_ref[0]

    @pl.when(i == 0)
    def _():
        gk_ref[...] = jnp.zeros_like(gk_ref)
        gv_ref[...] = jnp.zeros_like(gv_ref)

        @pl.when(core == 0)
        def _():
            for b in range(BLOCKS):
                k_sc[b * ROWS : (b + 1) * ROWS, :] = all_ref[b, base : base + ROWS, :]
                v_sc[b * ROWS : (b + 1) * ROWS, :] = other_ref[b]

        @pl.when(core != 0)
        def _():
            for b in range(BLOCKS):
                v_sc[b * ROWS : (b + 1) * ROWS, :] = all_ref[b, base : base + ROWS, :]
                k_sc[b * ROWS : (b + 1) * ROWS, :] = other_ref[b]

        count0 = jnp.zeros((1, ROWS), jnp.float32)
        count1 = jnp.zeros((1, ROWS), jnp.float32)
        for b in range(BLOCKS):
            ids_b = all_ref[b, base + ROWS : base + ROWS + TAIL, :].astype(jnp.float32)[:1]
            count0 += jnp.where(ids_b < 0.5, 1.0, 0.0)
            count1 += jnp.where(ids_b < 1.5, 1.0, 0.0)
        starts[0] = jnp.sum(count0).astype(jnp.int32)
        starts[1] = jnp.sum(count1).astype(jnp.int32)

    start1, start2 = starts[0], starts[1]

    def start_of(pos):
        return jnp.where(pos < start1, 0, jnp.where(pos < start2, start1, start2))

    first_block = start_of(i * ROWS) // ROWS
    blocks = jnp.minimum(i - first_block + 1, BAND // ROWS)

    def step(count):
        keys = count * ROWS
        q_pos = i * ROWS + lax.broadcasted_iota(jnp.int32, (1, ROWS), 1)
        q_pos = jnp.concatenate([q_pos] * heads, axis=1)
        q_start = start_of(q_pos)
        key_start = pl.multiple_of((i - (count - 1)) * ROWS, ROWS)
        band = pl.ds(key_start, keys)
        k = k_sc[band, :]
        v = v_sc[band, :]
        q = all_ref[i, : heads * ROWS, :]
        g = all_ref[i, heads * ROWS : 2 * heads * ROWS, :]
        k_pos = key_start + lax.broadcasted_iota(jnp.int32, (keys, m_cols), 0)
        scores = dot(k, q, NT) * EXP2_SCALE
        allowed = (k_pos <= q_pos) & (k_pos >= q_start)
        scores = jnp.where(allowed, scores, -jnp.inf)
        peak = jnp.max(scores, axis=0, keepdims=True)
        weights = jnp.exp2(scores - peak)
        inv = 1.0 / jnp.sum(weights, axis=0, keepdims=True)
        grad_probs = dot(v, g, NT)
        probs = weights * inv
        delta = jnp.sum(probs * grad_probs, axis=0, keepdims=True)
        probs_low = probs.astype(jnp.bfloat16)
        grad_scores = (probs * (grad_probs - delta)).astype(jnp.bfloat16)
        gv_ref[band, :] += dot(probs_low, g, NN)
        gk_ref[band, :] += dot(grad_scores, q, NN) * INV_ROOT
        gq = (dot(k, grad_scores, TN) * INV_ROOT).astype(jnp.bfloat16)
        for h in range(heads):
            gq_ref[:, h * HEAD : (h + 1) * HEAD] = gq[:, h * ROWS : (h + 1) * ROWS].T

    for count in range(1, BAND // ROWS + 1):
        pl.when(blocks == count)(lambda count=count: step(count))


def attention(where, everything, other):
    wide = (SEQ, HEAD)
    return pl.pallas_call(
        attention_body,
        grid=(BLOCKS,),
        in_specs=[SMEM, full(everything.shape), full(other.shape)],
        out_specs=[
            pl.BlockSpec((ROWS, HEADS * HEAD), lambda i: (i, 0)),
            full(wide),
            full(wide),
        ],
        out_shape=[
            jax.ShapeDtypeStruct((SEQ, HEADS * HEAD), jnp.bfloat16),
            jax.ShapeDtypeStruct(wide, jnp.float32),
            jax.ShapeDtypeStruct(wide, jnp.float32),
        ],
        scratch_shapes=[
            pltpu.VMEM(wide, jnp.bfloat16),
            pltpu.VMEM(wide, jnp.bfloat16),
            pltpu.SMEM((2,), jnp.int32),
        ],
        name="attention",
    )(where, everything, other)


def kernel(body, where, arrays, out_shape, name):
    many = isinstance(out_shape, list)
    vmem = pl.BlockSpec(memory_space=pltpu.VMEM)
    scalars = () if where is None else (where,)
    return pl.pallas_call(
        body,
        in_specs=[SMEM] * len(scalars) + [vmem] * len(arrays),
        out_specs=[vmem] * len(out_shape) if many else vmem,
        out_shape=out_shape,
        compiler_params=pltpu.CompilerParams(vmem_limit_bytes=SMALL_VMEM),
        name=name,
    )(*scalars, *arrays)


def project_part(side, where_ref, rows_ref, pieces, acc):
    x, y = where_ref[2], where_ref[3]
    for kx in range(4):
        part = (x - kx + 4) % 4
        for k in range(2):
            row = (y % 4) ^ (2 * k) ^ side
            at = pl.multiple_of((part * 2 + where_ref[0]) * 1024 + row * 256, 256)
            acc += dot(rows_ref[0, :, pl.ds(at, 256)], pieces[kx][k], NN)
    return acc


def near_body(where_ref, mine_ref, theirs_ref, p0, p1, p2, p3, own_ref, back_ref):
    zero = jnp.zeros((ROWS, RANK), jnp.float32)
    own_ref[...] = project_part(0, where_ref, mine_ref, (p0, p1, p2, p3), zero)
    back_ref[...] = project_part(0, where_ref, theirs_ref, (p0, p1, p2, p3), zero)


def far_body(where_ref, rows_ref, p0, p1, p2, p3, acc_ref, out_ref):
    out_ref[...] = project_part(1, where_ref, rows_ref, (p0, p1, p2, p3), acc_ref[...])


def outer_kv_body(p_ref, gk_ref, gv_ref, turned_ref, send_ref):
    turned_p = p_ref[...].reshape(SEQ, RANK).T
    turned_ref[...] = turned_p
    for side, ref in enumerate((gk_ref, gv_ref)):
        sums = dot(turned_p, ref[...].astype(jnp.bfloat16), NN).T.astype(jnp.bfloat16)
        for u in range(8):
            send_ref[u, side * 16 : (side + 1) * 16] = sums[u * 16 : (u + 1) * 16]


def outer_q_body(turned_ref, gq_ref, out_ref):
    out_ref[...] = dot(turned_ref[...], gq_ref[...], NN).astype(jnp.bfloat16)


def mix_body(q_ref, kv_ref, out_ref):
    sums = [
        kv_ref[2 * g].astype(jnp.float32) + kv_ref[2 * g + 1].astype(jnp.float32)
        for g in range(4)
    ]
    stacked = jnp.concatenate(sums, axis=0).astype(jnp.bfloat16)
    row = lax.broadcasted_iota(jnp.int32, (128, 128), 0)
    col = lax.broadcasted_iota(jnp.int32, (128, 128), 1)
    head, side, c = row // 32, (row // 16) % 2, row % 16
    order = jnp.where(col == side * 64 + c * 4 + head, 1.0, 0.0).astype(jnp.bfloat16)
    sums = dot(stacked, order, TN)
    out_ref[:, :, : HEADS * HEAD] = q_ref[...].reshape(64, 4, HEADS * HEAD)
    out_ref[:, :, HEADS * HEAD :] = sums.reshape(64, 4, HEAD).astype(jnp.bfloat16)


def turned(size, by):
    return [(i, (i + by) % size) for i in range(size)]


def core_swap(x):
    return lax.ppermute(x, "c", [(0, 1), (1, 0)])


def on_device(hidden_in, queries, keys, values, out_grad, doc_ids, flora_proj):
    core = lax.axis_index("c")
    zh = lax.axis_index("zh")
    x = lax.axis_index("x")
    y = lax.axis_index("y")
    where = jnp.stack([core, zh, x, y]).astype(jnp.int32)
    low = jnp.bfloat16

    rows = lax.dynamic_slice_in_dim(flora_proj, (y % 4) * 256, 256, 0)
    rows = lax.ppermute(
        rows, ("x", "zh"), [(a * 4 + b, b * 4 + a) for a in range(4) for b in range(4)]
    )
    sent = pack(queries, out_grad, keys, values, doc_ids)
    theirs = core_swap(hidden_in)
    rows, sent, theirs = lax.optimization_barrier((rows, sent, theirs))
    everything = lax.all_to_all(sent, ("zh", "c"), 0, 0, tiled=True)

    def spread(piece):
        return [piece] + [lax.ppermute(piece, "x", turned(4, k)) for k in (1, 3, 2)]

    near = jnp.stack([rows, lax.ppermute(rows, "y", [(i, i ^ 2) for i in range(8)])])
    far = lax.ppermute(near, "y", [(i, i ^ 1) for i in range(8)])
    half = jax.ShapeDtypeStruct((ROWS, RANK), jnp.float32)

    def pieces(piece):
        one, back, three, two = (*spread(piece),)
        return one, back, two, three

    own, back = kernel(
        near_body, where, [hidden_in, theirs, *pieces(near)], [half, half], "project_near"
    )
    far = pieces(far)
    back = kernel(far_body, where, [theirs, *far, back], half, "project_back")
    own, _ = lax.optimization_barrier((own, back))
    own = kernel(far_body, where, [hidden_in, *far, own], half, "project_own")
    projected = (own + core_swap(back)).astype(low)
    other = core_swap(everything[:, KV_AT : KV_AT + ROWS, :])
    all_projected = lax.all_to_all(
        jnp.broadcast_to(projected, (8, ROWS, RANK)), ("zh", "c"), 0, 0, tiled=True
    )
    where, _ = lax.optimization_barrier((where, projected))
    gq, gk, gv = attention(where, everything, other)
    turned_p, kv_part = kernel(
        outer_kv_body,
        None,
        [all_projected, gk, gv],
        [jax.ShapeDtypeStruct((RANK, SEQ), low), jax.ShapeDtypeStruct((8, 32, RANK), low)],
        "outer_kv",
    )
    kv_part = lax.all_to_all(kv_part, ("zh", "c"), 0, 0, tiled=True)
    q_part = kernel(
        outer_q_body,
        None,
        [turned_p, gq],
        jax.ShapeDtypeStruct((RANK, HEADS * HEAD), low),
        "outer_q",
    )
    local = kernel(
        mix_body,
        None,
        [q_part, kv_part],
        jax.ShapeDtypeStruct((64, 4, HEADS * HEAD + HEAD), low),
        "mix",
    )
    parts = lax.all_to_all(local, ("x", "y", "zl"), 0, 0, tiled=True)
    sums = jnp.sum(parts.astype(jnp.float32), axis=0)
    at = HEADS * HEAD
    return sums[:, :at], sums[:, at : at + 64], sums[:, at + 64 :]


def solution(mesh):
    fine = Mesh(np.asarray(mesh.devices).reshape(4, 8, 2, 4, 2), ("x", "y", "zl", "zh", "c"))
    dp = ("x", "y", "zl")
    uly = ("zh", "c")
    placed = (P(dp, uly, None),) * 5 + (P(dp, uly), P(uly, None))
    return jax.shard_map(
        on_device,
        mesh=fine,
        in_specs=placed,
        out_specs=(P(dp, uly), P(dp, uly), P(dp, uly)),
        check_vma=False,
    )
```

```python
import math

import jax
import jax.numpy as jnp
import numpy as np
from jax import lax
from jax.experimental import pallas as pl
from jax.experimental.pallas import tpu as pltpu
from jax.sharding import Mesh
from jax.sharding import PartitionSpec as P


HEAD = 128
ROWS = 128
RANK = 256
SEQ = 1024
BLOCKS = SEQ // ROWS
BAND = 640
INV_ROOT = 1.0 / math.sqrt(HEAD)
EXP2_SCALE = INV_ROOT * math.log2(math.e)
HEADS = 4
TAIL = 16
KV_AT = 2 * HEADS * ROWS
SMALL_VMEM = 16 * 2**20

NT = (((1,), (1,)), ((), ()))
TN = (((0,), (0,)), ((), ()))
NN = (((1,), (0,)), ((), ()))


def dot(a, b, dims):
    return lax.dot_general(a, b, dims, preferred_element_type=jnp.float32)


def full(shape):
    return pl.BlockSpec(shape, lambda *_: (0,) * len(shape))


SMEM = pl.BlockSpec(memory_space=pltpu.SMEM)


def pack_body(q_ref, g_ref, k_ref, v_ref, ids_ref, out_ref):
    for p in range(2):
        for h in range(HEADS):
            cols = slice((p * HEADS + h) * HEAD, (p * HEADS + h + 1) * HEAD)
            out_ref[p, h * ROWS : (h + 1) * ROWS, :] = q_ref[0, :, cols]
            out_ref[p, (HEADS + h) * ROWS : (HEADS + h + 1) * ROWS, :] = g_ref[0, :, cols]
        out_ref[p, KV_AT : KV_AT + ROWS, :] = (v_ref if p else k_ref)[0]
        out_ref[p, KV_AT + ROWS :, :] = jnp.broadcast_to(
            ids_ref[...].astype(jnp.float32), (TAIL, ROWS)
        ).astype(jnp.bfloat16)


def pack(queries, out_grad, keys, values, ids):
    wide = pl.BlockSpec((1, ROWS, 2 * HEADS * HEAD), lambda u: (0, 0, u))
    thin = pl.BlockSpec((1, ROWS, HEAD), lambda u: (0, 0, u))
    return pl.pallas_call(
        pack_body,
        grid=(4,),
        in_specs=[wide, wide, thin, thin, full((1, ROWS))],
        out_specs=pl.BlockSpec((2, KV_AT + ROWS + TAIL, HEAD), lambda u: (u, 0, 0)),
        out_shape=jax.ShapeDtypeStruct((8, KV_AT + ROWS + TAIL, HEAD), jnp.bfloat16),
        name="pack",
    )(queries, out_grad, keys, values, ids)


def attention_body(
    where_ref, all_ref, other_ref, gq_ref, gkv_ref, gk_ref, gv_ref, k_sc, v_sc, starts
):
    heads = HEADS
    i = pl.program_id(0)
    m_cols = heads * ROWS
    base = KV_AT
    core = where_ref[0]

    @pl.when(i == 0)
    def _():
        gk_ref[...] = jnp.zeros_like(gk_ref)
        gv_ref[...] = jnp.zeros_like(gv_ref)

        @pl.when(core == 0)
        def _():
            for b in range(BLOCKS):
                k_sc[b * ROWS : (b + 1) * ROWS, :] = all_ref[b, base : base + ROWS, :]
                v_sc[b * ROWS : (b + 1) * ROWS, :] = other_ref[b]

        @pl.when(core != 0)
        def _():
            for b in range(BLOCKS):
                v_sc[b * ROWS : (b + 1) * ROWS, :] = all_ref[b, base : base + ROWS, :]
                k_sc[b * ROWS : (b + 1) * ROWS, :] = other_ref[b]

        count0 = jnp.zeros((1, ROWS), jnp.float32)
        count1 = jnp.zeros((1, ROWS), jnp.float32)
        for b in range(BLOCKS):
            ids_b = all_ref[b, base + ROWS : base + ROWS + TAIL, :].astype(jnp.float32)[:1]
            count0 += jnp.where(ids_b < 0.5, 1.0, 0.0)
            count1 += jnp.where(ids_b < 1.5, 1.0, 0.0)
        starts[0] = jnp.sum(count0).astype(jnp.int32)
        starts[1] = jnp.sum(count1).astype(jnp.int32)

    start1, start2 = starts[0], starts[1]

    def start_of(pos):
        return jnp.where(pos < start1, 0, jnp.where(pos < start2, start1, start2))

    first_block = start_of(i * ROWS) // ROWS
    blocks = jnp.minimum(i - first_block + 1, BAND // ROWS)

    def step(count):
        keys = count * ROWS
        q_pos = i * ROWS + lax.broadcasted_iota(jnp.int32, (1, ROWS), 1)
        q_pos = jnp.concatenate([q_pos] * heads, axis=1)
        q_start = start_of(q_pos)
        key_start = pl.multiple_of((i - (count - 1)) * ROWS, ROWS)
        band = pl.ds(key_start, keys)
        k = k_sc[band, :]
        v = v_sc[band, :]
        q = all_ref[i, : heads * ROWS, :]
        g = all_ref[i, heads * ROWS : 2 * heads * ROWS, :]
        k_pos = key_start + lax.broadcasted_iota(jnp.int32, (keys, m_cols), 0)
        scores = dot(k, q, NT) * EXP2_SCALE
        allowed = (k_pos <= q_pos) & (k_pos >= q_start)
        scores = jnp.where(allowed, scores, -jnp.inf)
        peak = jnp.max(scores, axis=0, keepdims=True)
        weights = jnp.exp2(scores - peak)
        inv = 1.0 / jnp.sum(weights, axis=0, keepdims=True)
        grad_probs = dot(v, g, NT)
        probs = weights * inv
        delta = jnp.sum(probs * grad_probs, axis=0, keepdims=True)
        probs_low = probs.astype(jnp.bfloat16)
        grad_scores = (probs * (grad_probs - delta)).astype(jnp.bfloat16)
        gv_ref[band, :] += dot(probs_low, g, NN)
        gk_ref[band, :] += dot(grad_scores, q, NN)
        gq = (dot(k, grad_scores, TN) * INV_ROOT).astype(jnp.bfloat16)
        for h in range(heads):
            gq_ref[:, h * HEAD : (h + 1) * HEAD] = gq[:, h * ROWS : (h + 1) * ROWS].T

    for count in range(1, BAND // ROWS + 1):
        pl.when(blocks == count)(lambda count=count: step(count))

    @pl.when(i == BLOCKS - 1)
    def _():
        gkv_ref[:, :HEAD] = (gk_ref[...] * INV_ROOT).astype(jnp.bfloat16)
        gkv_ref[:, HEAD:] = gv_ref[...].astype(jnp.bfloat16)


def attention(where, everything, other):
    wide = (SEQ, HEAD)
    return pl.pallas_call(
        attention_body,
        grid=(BLOCKS,),
        in_specs=[SMEM, full(everything.shape), full(other.shape)],
        out_specs=[
            pl.BlockSpec((ROWS, HEADS * HEAD), lambda i: (i, 0)),
            full((SEQ, 2 * HEAD)),
        ],
        out_shape=[
            jax.ShapeDtypeStruct((SEQ, HEADS * HEAD), jnp.bfloat16),
            jax.ShapeDtypeStruct((SEQ, 2 * HEAD), jnp.bfloat16),
        ],
        scratch_shapes=[
            pltpu.VMEM(wide, jnp.float32),
            pltpu.VMEM(wide, jnp.float32),
            pltpu.VMEM(wide, jnp.bfloat16),
            pltpu.VMEM(wide, jnp.bfloat16),
            pltpu.SMEM((2,), jnp.int32),
        ],
        name="attention",
    )(where, everything, other)


def kernel(body, where, arrays, out_shape):
    many = isinstance(out_shape, list)
    vmem = pl.BlockSpec(memory_space=pltpu.VMEM)
    scalars = () if where is None else (where,)
    return pl.pallas_call(
        body,
        in_specs=[SMEM] * len(scalars) + [vmem] * len(arrays),
        out_specs=[vmem] * len(out_shape) if many else vmem,
        out_shape=out_shape,
        compiler_params=pltpu.CompilerParams(vmem_limit_bytes=SMALL_VMEM),
    )(*scalars, *arrays)


def project_part(side, where_ref, rows_ref, pieces, acc):
    x, y = where_ref[2], where_ref[3]
    for kx in range(4):
        part = (x - kx + 4) % 4
        for k in range(2):
            row = (y % 4) ^ (2 * k) ^ side
            at = pl.multiple_of((part * 2 + where_ref[0]) * 1024 + row * 256, 256)
            acc += dot(rows_ref[0, :, pl.ds(at, 256)], pieces[kx][k], NN)
    return acc


def near_body(where_ref, mine_ref, theirs_ref, p0, p1, p2, p3, own_ref, back_ref):
    zero = jnp.zeros((ROWS, RANK), jnp.float32)
    own_ref[...] = project_part(0, where_ref, mine_ref, (p0, p1, p2, p3), zero)
    back_ref[...] = project_part(0, where_ref, theirs_ref, (p0, p1, p2, p3), zero)


def far_body(where_ref, rows_ref, p0, p1, p2, p3, acc_ref, out_ref):
    out_ref[...] = project_part(1, where_ref, rows_ref, (p0, p1, p2, p3), acc_ref[...])


def outer_kv_body(p_ref, gkv_ref, turned_ref, send_ref):
    turned_p = p_ref[...].reshape(SEQ, RANK).T
    turned_ref[...] = turned_p
    sums = dot(turned_p, gkv_ref[...], NN).T.astype(jnp.bfloat16)
    for side in range(2):
        for u in range(8):
            at = side * HEAD + u * 16
            send_ref[u, side * 16 : (side + 1) * 16] = sums[at : at + 16]


def outer_q_body(turned_ref, gq_ref, out_ref):
    out_ref[...] = dot(turned_ref[...], gq_ref[...], NN).astype(jnp.bfloat16)


def mix_body(q_ref, kv_ref, out_ref):
    sums = [
        kv_ref[2 * g].astype(jnp.float32) + kv_ref[2 * g + 1].astype(jnp.float32)
        for g in range(4)
    ]
    stacked = jnp.concatenate(sums, axis=0).astype(jnp.bfloat16)
    row = lax.broadcasted_iota(jnp.int32, (128, 128), 0)
    col = lax.broadcasted_iota(jnp.int32, (128, 128), 1)
    head, side, c = row // 32, (row // 16) % 2, row % 16
    order = jnp.where(col == side * 64 + c * 4 + head, 1.0, 0.0).astype(jnp.bfloat16)
    sums = dot(stacked, order, TN)
    out_ref[:, :, : HEADS * HEAD] = q_ref[...].reshape(64, 4, HEADS * HEAD)
    out_ref[:, :, HEADS * HEAD :] = sums.reshape(64, 4, HEAD).astype(jnp.bfloat16)


def turned(size, by):
    return [(i, (i + by) % size) for i in range(size)]


def core_swap(x):
    return lax.ppermute(x, "c", [(0, 1), (1, 0)])


def backward(hidden_in, queries, keys, values, out_grad, doc_ids, flora_proj):
    core = lax.axis_index("c")
    zh = lax.axis_index("zh")
    x = lax.axis_index("x")
    y = lax.axis_index("y")
    where = jnp.stack([core, zh, x, y]).astype(jnp.int32)
    low = jnp.bfloat16

    rows = lax.dynamic_slice_in_dim(flora_proj, (y % 4) * 256, 256, 0)
    rows, queries, doc_ids = lax.optimization_barrier((rows, queries, doc_ids))
    rows = lax.ppermute(
        rows, ("x", "zh"), [(a * 4 + b, b * 4 + a) for a in range(4) for b in range(4)]
    )
    sent = pack(queries, out_grad, keys, values, doc_ids)
    everything = lax.all_to_all(sent, ("zh", "c"), 0, 0, tiled=True)

    def spread(piece):
        return [piece] + [lax.ppermute(piece, "x", turned(4, k)) for k in (1, 3, 2)]

    near = jnp.stack([rows, lax.ppermute(rows, "y", [(i, i ^ 2) for i in range(8)])])
    far = lax.ppermute(near, "y", [(i, i ^ 1) for i in range(8)])
    theirs = core_swap(hidden_in)
    half = jax.ShapeDtypeStruct((ROWS, RANK), jnp.float32)

    def pieces(piece):
        one, back, three, two = (*spread(piece),)
        return one, back, two, three

    near = pieces(near)
    far = pieces(far)
    own, back = kernel(near_body, where, [hidden_in, theirs, *near], [half, half])
    back = kernel(far_body, where, [theirs, *far, back], half)
    own, _ = lax.optimization_barrier((own, back))
    own = kernel(far_body, where, [hidden_in, *far, own], half)
    projected = (own + core_swap(back)).astype(low)
    other = core_swap(everything[:, KV_AT : KV_AT + ROWS, :])
    copies = jnp.broadcast_to(projected, (8, ROWS, RANK))
    all_projected = lax.all_to_all(copies, ("zh", "c"), 0, 0, tiled=True)
    where, _ = lax.optimization_barrier((where, projected))
    gq, gkv = attention(where, everything, other)
    turned_p, kv_part = kernel(
        outer_kv_body,
        None,
        [all_projected, gkv],
        [jax.ShapeDtypeStruct((RANK, SEQ), low), jax.ShapeDtypeStruct((8, 32, RANK), low)],
    )
    kv_part = lax.all_to_all(kv_part, ("zh", "c"), 0, 0, tiled=True)
    q_part = kernel(
        outer_q_body,
        None,
        [turned_p, gq],
        jax.ShapeDtypeStruct((RANK, HEADS * HEAD), low),
    )
    local = kernel(
        mix_body,
        None,
        [q_part, kv_part],
        jax.ShapeDtypeStruct((64, 4, HEADS * HEAD + HEAD), low),
    )
    parts = lax.all_to_all(local, ("x", "y", "zl"), 0, 0, tiled=True)
    sums = jnp.sum(parts.astype(jnp.float32), axis=0)
    at = HEADS * HEAD
    return sums[:, :at], sums[:, at : at + 64], sums[:, at + 64 :]


def solution(mesh):
    fine = Mesh(np.asarray(mesh.devices).reshape(4, 8, 2, 4, 2), ("x", "y", "zl", "zh", "c"))
    dp = ("x", "y", "zl")
    uly = ("zh", "c")
    placed = (P(dp, uly, None),) * 5 + (P(dp, uly), P(uly, None))
    return jax.shard_map(
        backward,
        mesh=fine,
        in_specs=placed,
        out_specs=(P(dp, uly), P(dp, uly), P(dp, uly)),
        check_vma=False,
    )
```

```python
import math

import jax
import jax.numpy as jnp
import numpy as np
from jax import lax
from jax.experimental import pallas as pl
from jax.experimental.pallas import tpu as pltpu
from jax.sharding import Mesh
from jax.sharding import PartitionSpec as P


HEAD = 128
ROWS = 128
RANK = 256
SEQ = 1024
BLOCKS = SEQ // ROWS
BAND = 640
INV_ROOT = 1.0 / math.sqrt(HEAD)
EXP2_SCALE = INV_ROOT * math.log2(math.e)
HEADS = 4
TAIL = 16
KV_AT = 2 * HEADS * ROWS
SMALL_VMEM = 16 * 2**20
PEERS_AT_ONCE = 2

NT = (((1,), (1,)), ((), ()))
TN = (((0,), (0,)), ((), ()))
NN = (((1,), (0,)), ((), ()))


def dot(a, b, dims):
    return lax.dot_general(a, b, dims, preferred_element_type=jnp.float32)


def full(shape):
    return pl.BlockSpec(shape, lambda *_: (0,) * len(shape))


SMEM = pl.BlockSpec(memory_space=pltpu.SMEM)


def pack_body(q_ref, g_ref, k_ref, v_ref, ids_ref, out_ref):
    ids = jnp.broadcast_to(ids_ref[...].astype(jnp.float32), (TAIL, ROWS)).astype(jnp.bfloat16)
    for p in range(PEERS_AT_ONCE):
        for h in range(HEADS):
            cols = slice((p * HEADS + h) * HEAD, (p * HEADS + h + 1) * HEAD)
            out_ref[p, h * ROWS : (h + 1) * ROWS, :] = q_ref[0, :, cols]
            out_ref[p, (HEADS + h) * ROWS : (HEADS + h + 1) * ROWS, :] = g_ref[0, :, cols]
        cols = slice((p // 2) * HEAD, (p // 2 + 1) * HEAD)
        out_ref[p, KV_AT : KV_AT + ROWS, :] = (v_ref if p % 2 else k_ref)[0, :, cols]
        out_ref[p, KV_AT + ROWS :, :] = ids


def pack(queries, out_grad, keys, values, ids):
    n = PEERS_AT_ONCE
    wide = pl.BlockSpec((1, ROWS, n * HEADS * HEAD), lambda u: (0, 0, u))
    thin = pl.BlockSpec((1, ROWS, n // 2 * HEAD), lambda u: (0, 0, u))
    return pl.pallas_call(
        pack_body,
        grid=(8 // n,),
        in_specs=[wide, wide, thin, thin, full((1, ROWS))],
        out_specs=pl.BlockSpec((n, KV_AT + ROWS + TAIL, HEAD), lambda u: (u, 0, 0)),
        out_shape=jax.ShapeDtypeStruct((8, KV_AT + ROWS + TAIL, HEAD), jnp.bfloat16),
        name="pack",
    )(queries, out_grad, keys, values, ids)


def attention_body(
    where_ref, all_ref, other_ref, gq_ref, gkv_ref, gk_ref, gv_ref, k_sc, v_sc, starts
):
    heads = HEADS
    i = pl.program_id(0)
    m_cols = heads * ROWS
    base = KV_AT
    core = where_ref[0]

    @pl.when(i == 0)
    def _():
        gk_ref[...] = jnp.zeros_like(gk_ref)
        gv_ref[...] = jnp.zeros_like(gv_ref)

        @pl.when(core == 0)
        def _():
            for b in range(BLOCKS):
                k_sc[b * ROWS : (b + 1) * ROWS, :] = all_ref[b, base : base + ROWS, :]
                v_sc[b * ROWS : (b + 1) * ROWS, :] = other_ref[b]

        @pl.when(core != 0)
        def _():
            for b in range(BLOCKS):
                v_sc[b * ROWS : (b + 1) * ROWS, :] = all_ref[b, base : base + ROWS, :]
                k_sc[b * ROWS : (b + 1) * ROWS, :] = other_ref[b]

        count0 = jnp.zeros((1, ROWS), jnp.float32)
        count1 = jnp.zeros((1, ROWS), jnp.float32)
        for b in range(BLOCKS):
            ids_b = all_ref[b, base + ROWS : base + ROWS + TAIL, :].astype(jnp.float32)[:1]
            count0 += jnp.where(ids_b < 0.5, 1.0, 0.0)
            count1 += jnp.where(ids_b < 1.5, 1.0, 0.0)
        starts[0] = jnp.sum(count0).astype(jnp.int32)
        starts[1] = jnp.sum(count1).astype(jnp.int32)

    start1, start2 = starts[0], starts[1]

    def start_of(pos):
        return jnp.where(pos < start1, 0, jnp.where(pos < start2, start1, start2))

    first_block = start_of(i * ROWS) // ROWS
    blocks = jnp.minimum(i - first_block + 1, BAND // ROWS)

    def step(count):
        keys = count * ROWS
        q_pos = i * ROWS + lax.broadcasted_iota(jnp.int32, (1, ROWS), 1)
        q_pos = jnp.concatenate([q_pos] * heads, axis=1)
        q_start = start_of(q_pos)
        key_start = pl.multiple_of((i - (count - 1)) * ROWS, ROWS)
        band = pl.ds(key_start, keys)
        k = k_sc[band, :]
        v = v_sc[band, :]
        q = all_ref[i, : heads * ROWS, :]
        g = all_ref[i, heads * ROWS : 2 * heads * ROWS, :]
        k_pos = key_start + lax.broadcasted_iota(jnp.int32, (keys, m_cols), 0)
        scores = dot(k, q, NT) * EXP2_SCALE
        allowed = (k_pos <= q_pos) & (k_pos >= q_start)
        scores = jnp.where(allowed, scores, -jnp.inf)
        peak = jnp.max(scores, axis=0, keepdims=True)
        weights = jnp.exp2(scores - peak)
        inv = 1.0 / jnp.sum(weights, axis=0, keepdims=True)
        grad_probs = dot(v, g, NT)
        probs = weights * inv
        delta = jnp.sum(probs * grad_probs, axis=0, keepdims=True)
        probs_low = probs.astype(jnp.bfloat16)
        grad_scores = (probs * (grad_probs - delta)).astype(jnp.bfloat16)
        gv_ref[band, :] += dot(probs_low, g, NN)
        gk_ref[band, :] += dot(grad_scores, q, NN)
        gq = (dot(k, grad_scores, TN) * INV_ROOT).astype(jnp.bfloat16)
        for h in range(heads):
            gq_ref[:, h * HEAD : (h + 1) * HEAD] = gq[:, h * ROWS : (h + 1) * ROWS].T

    for count in range(1, BAND // ROWS + 1):
        pl.when(blocks == count)(lambda count=count: step(count))

    @pl.when(i == BLOCKS - 1)
    def _():
        gkv_ref[:, :HEAD] = (gk_ref[...] * INV_ROOT).astype(jnp.bfloat16)
        gkv_ref[:, HEAD:] = gv_ref[...].astype(jnp.bfloat16)


def attention(where, everything, other):
    wide = (SEQ, HEAD)
    return pl.pallas_call(
        attention_body,
        grid=(BLOCKS,),
        in_specs=[SMEM, full(everything.shape), full(other.shape)],
        out_specs=[
            pl.BlockSpec((ROWS, HEADS * HEAD), lambda i: (i, 0)),
            full((SEQ, 2 * HEAD)),
        ],
        out_shape=[
            jax.ShapeDtypeStruct((SEQ, HEADS * HEAD), jnp.bfloat16),
            jax.ShapeDtypeStruct((SEQ, 2 * HEAD), jnp.bfloat16),
        ],
        scratch_shapes=[
            pltpu.VMEM(wide, jnp.float32),
            pltpu.VMEM(wide, jnp.float32),
            pltpu.VMEM(wide, jnp.bfloat16),
            pltpu.VMEM(wide, jnp.bfloat16),
            pltpu.SMEM((2,), jnp.int32),
        ],
        name="attention",
    )(where, everything, other)


def kernel(body, where, arrays, out_shape):
    many = isinstance(out_shape, list)
    vmem = pl.BlockSpec(memory_space=pltpu.VMEM)
    scalars = () if where is None else (where,)
    return pl.pallas_call(
        body,
        in_specs=[SMEM] * len(scalars) + [vmem] * len(arrays),
        out_specs=[vmem] * len(out_shape) if many else vmem,
        out_shape=out_shape,
        compiler_params=pltpu.CompilerParams(vmem_limit_bytes=SMALL_VMEM),
    )(*scalars, *arrays)


def project_part(side, where_ref, rows_ref, pieces, acc):
    x, y = where_ref[2], where_ref[3]
    for kx in range(4):
        part = (x - kx + 4) % 4
        for k in range(2):
            row = (y % 4) ^ (2 * k) ^ side
            at = pl.multiple_of((part * 2 + where_ref[0]) * 1024 + row * 256, 256)
            acc += dot(rows_ref[0, :, pl.ds(at, 256)], pieces[kx][k], NN)
    return acc


def near_body(where_ref, mine_ref, theirs_ref, p0, p1, p2, p3, own_ref, back_ref):
    zero = jnp.zeros((ROWS, RANK), jnp.float32)
    own_ref[...] = project_part(0, where_ref, mine_ref, (p0, p1, p2, p3), zero)
    back_ref[...] = project_part(0, where_ref, theirs_ref, (p0, p1, p2, p3), zero)


def far_body(where_ref, rows_ref, p0, p1, p2, p3, acc_ref, out_ref):
    out_ref[...] = project_part(1, where_ref, rows_ref, (p0, p1, p2, p3), acc_ref[...])


def finish_body(own_ref, got_ref, out_ref):
    projected = (own_ref[...] + got_ref[...]).astype(jnp.bfloat16)
    for u in range(8):
        out_ref[u] = projected


def outer_kv_body(p_ref, gkv_ref, turned_ref, send_ref):
    turned_p = p_ref[...].reshape(SEQ, RANK).T
    turned_ref[...] = turned_p
    sums = dot(turned_p, gkv_ref[...], NN).T.astype(jnp.bfloat16)
    for side in range(2):
        for u in range(8):
            at = side * HEAD + u * 16
            send_ref[u, side * 16 : (side + 1) * 16] = sums[at : at + 16]


def outer_q_body(turned_ref, gq_ref, out_ref):
    out_ref[...] = dot(turned_ref[...], gq_ref[...], NN).astype(jnp.bfloat16)


def mix_body(q_ref, kv_ref, out_ref):
    sums = [
        kv_ref[2 * g].astype(jnp.float32) + kv_ref[2 * g + 1].astype(jnp.float32)
        for g in range(4)
    ]
    stacked = jnp.concatenate(sums, axis=0).astype(jnp.bfloat16)
    row = lax.broadcasted_iota(jnp.int32, (128, 128), 0)
    col = lax.broadcasted_iota(jnp.int32, (128, 128), 1)
    head, side, c = row // 32, (row // 16) % 2, row % 16
    order = jnp.where(col == side * 64 + c * 4 + head, 1.0, 0.0).astype(jnp.bfloat16)
    sums = dot(stacked, order, TN)
    out_ref[:, :, : HEADS * HEAD] = q_ref[...].reshape(64, 4, HEADS * HEAD)
    out_ref[:, :, HEADS * HEAD :] = sums.reshape(64, 4, HEAD).astype(jnp.bfloat16)


def turned(size, by):
    return [(i, (i + by) % size) for i in range(size)]


def core_swap(x):
    return lax.ppermute(x, "c", [(0, 1), (1, 0)])


def backward(hidden_in, queries, keys, values, out_grad, doc_ids, flora_proj):
    core = lax.axis_index("c")
    zh = lax.axis_index("zh")
    x = lax.axis_index("x")
    y = lax.axis_index("y")
    where = jnp.stack([core, zh, x, y]).astype(jnp.int32)
    low = jnp.bfloat16

    rows = lax.dynamic_slice_in_dim(flora_proj, (y % 4) * 256, 256, 0)
    rows, queries, doc_ids = lax.optimization_barrier((rows, queries, doc_ids))
    rows = lax.ppermute(
        rows, ("x", "zh"), [(a * 4 + b, b * 4 + a) for a in range(4) for b in range(4)]
    )
    sent = pack(queries, out_grad, keys, values, doc_ids)
    everything = lax.all_to_all(sent, ("zh", "c"), 0, 0, tiled=True)

    def spread(piece):
        return [piece] + [lax.ppermute(piece, "x", turned(4, k)) for k in (1, 3, 2)]

    near = jnp.stack([rows, lax.ppermute(rows, "y", [(i, i ^ 2) for i in range(8)])])
    far = lax.ppermute(near, "y", [(i, i ^ 1) for i in range(8)])
    theirs = core_swap(hidden_in)
    half = jax.ShapeDtypeStruct((ROWS, RANK), jnp.float32)

    def pieces(piece):
        one, back, three, two = (*spread(piece),)
        return one, back, two, three

    near = pieces(near)
    far = pieces(far)
    own, back = kernel(near_body, where, [hidden_in, theirs, *near], [half, half])
    back = kernel(far_body, where, [theirs, *far, back], half)
    own, _ = lax.optimization_barrier((own, back))
    own = kernel(far_body, where, [hidden_in, *far, own], half)
    copies = kernel(
        finish_body,
        None,
        [own, core_swap(back)],
        jax.ShapeDtypeStruct((8, ROWS, RANK), low),
    )
    other = core_swap(everything[:, KV_AT : KV_AT + ROWS, :])
    all_projected = lax.all_to_all(copies, ("zh", "c"), 0, 0, tiled=True)
    where, _ = lax.optimization_barrier((where, copies))
    gq, gkv = attention(where, everything, other)
    turned_p, kv_part = kernel(
        outer_kv_body,
        None,
        [all_projected, gkv],
        [jax.ShapeDtypeStruct((RANK, SEQ), low), jax.ShapeDtypeStruct((8, 32, RANK), low)],
    )
    kv_part = lax.all_to_all(kv_part, ("zh", "c"), 0, 0, tiled=True)
    q_part = kernel(
        outer_q_body,
        None,
        [turned_p, gq],
        jax.ShapeDtypeStruct((RANK, HEADS * HEAD), low),
    )
    local = kernel(
        mix_body,
        None,
        [q_part, kv_part],
        jax.ShapeDtypeStruct((64, 4, HEADS * HEAD + HEAD), low),
    )
    parts = lax.all_to_all(local, ("x", "y", "zl"), 0, 0, tiled=True)
    at = HEADS * HEAD

    def summed(columns):
        return jnp.sum(columns.astype(jnp.float32), axis=0)

    return (
        summed(parts[:, :, :at]),
        summed(parts[:, :, at : at + 64]),
        summed(parts[:, :, at + 64 :]),
    )


def solution(mesh):
    fine = Mesh(np.asarray(mesh.devices).reshape(4, 8, 2, 4, 2), ("x", "y", "zl", "zh", "c"))
    dp = ("x", "y", "zl")
    uly = ("zh", "c")
    placed = (P(dp, uly, None),) * 5 + (P(dp, uly), P(uly, None))
    return jax.shard_map(
        backward,
        mesh=fine,
        in_specs=placed,
        out_specs=(P(dp, uly), P(dp, uly), P(dp, uly)),
        check_vma=False,
    )
```
